128 devices in a mesh: req: 16 (over z, x), mlp: 8 (over y, core).
Axes of the slice: x: 4, y: 4, z: 4, core: 2. Of those that a mesh axis runs over, the one named last changes fastest.
Arguments:
- tokens: bfloat16 [65536, 1024], P(('req', 'mlp')), may hold values from -72 to 72
- attend_weight: bfloat16 [1024, 3072], replicated, may hold values from -0.1875 to 0.1875
- output_weight: bfloat16 [1024, 1024], replicated, may hold values from -0.1875 to 0.1875
- attend_gain: float32 [1024], replicated, may hold values from 0.1 to 1.9
- up_weight: bfloat16 [1024, 4096], P(None, 'mlp'), may hold values from -0.1875 to 0.1875
- down_weight: bfloat16 [1024, 4096], P(None, 'mlp'), may hold values from -0.09375 to 0.09375
- mlp_gain: float32 [1024], replicated, may hold values from 0.1 to 1.9
- embed_weight: bfloat16 [1024, 128], replicated, may hold values from -0.1875 to 0.1875
- query_length: int32 [512], P(('req', 'mlp')), may hold values from 1 to 128, 49152 in all
- documents: bfloat16 [128, 256, 128], P('req', 'mlp'), may hold values from -0.54 to 0.54
- document_length: int32 [128], P('req'), may hold values from 1 to 256, 16512 in all
- candidates: int32 [512, 8], P(('req', 'mlp')), may hold values from 0 to 127
Outputs:
- embedded: bfloat16 [65536, 128], P(('req', 'mlp'))
- scores: float32 [512, 8], P(('req', 'mlp'))
The draws below stay inside these ranges and needn't reach their ends.
All inputs are finite; a program needn't handle non-finite values. No bound on the sum of `query_length` or of `document_length` on one device may be relied on, other than what follows from the above.
Results may differ from the reference program's by a relative error of at most 0.015.
The reference program's roundings to bfloat16 on the way (of `packed`, `probs`, `context`, `normed`, `inner` and `layer_out`) count: a program that leaves them out, or rounds other values in their place, can miss the bound.
Values may be sent and summed in bfloat16 or wider, within the bound.
No kernel may reach another device: no remote copies, remote signals or barrier semaphores. Data moves between devices by JAX's collectives and lax.ppermute only.
A program may use at most 128 MiB of HBM per device.

```python
import math
import jax
import jax.numpy as jnp
import numpy as np
from jax import lax

D = 1024
HEADS = 16
HD = 64
FF = 4096
P_SIZE = 128
SEQ = 128
DLEN = 256
CAND = 8
REQS = 512
TOKENS = 65536
DOCS = 128


def draw_tokens(key, part):
    noise_key = jax.random.fold_in(key, 11)
    topic_key = jax.random.fold_in(key, 13)
    groups = TOKENS // SEQ
    noise = jax.random.truncated_normal(noise_key, -3.0, 3.0, (groups, SEQ, D), jnp.float32)
    topic = jax.random.truncated_normal(topic_key, -3.0, 3.0, (groups, 1, D), jnp.float32)
    base = (noise + topic).reshape(TOKENS, D)
    return base.astype(jnp.bfloat16)


def draw_documents(key, part):
    noise_key = jax.random.fold_in(key, 21)
    head_key = jax.random.fold_in(key, 23)
    tail_key = jax.random.fold_in(key, 29)
    noise = 0.08 * jax.random.truncated_normal(noise_key, -6.0, 6.0, (DOCS, DLEN, P_SIZE), jnp.float32)
    weight_topic = 2.0 / math.sqrt(P_SIZE)
    head = jnp.where(jax.random.bernoulli(head_key, 0.5, (DOCS, 1, P_SIZE)), weight_topic, -weight_topic)
    tail = jnp.where(jax.random.bernoulli(tail_key, 0.5, (DOCS, 1, P_SIZE)), weight_topic, -weight_topic)
    late = (jnp.arange(DLEN) >= DLEN * 3 // 4)[None, :, None]
    topic = jnp.where(late, tail, head)
    return jnp.clip(noise + topic, -0.54, 0.54).astype(jnp.bfloat16)


def touch_ends(result, key, least, largest):
    longest = result.shape.index(max(result.shape))
    spots = []
    for shift in (0, 1):
        where = [jax.random.randint(jax.random.fold_in(key, axis), (), 0, length) for axis, length in enumerate(result.shape)]
        where[longest] = (where[longest] + shift) % result.shape[longest]
        spots.append(tuple(where))
    return result.at[spots[0]].set(least).at[spots[1]].set(largest)


def shard_levels(stream_key, shape, pieces, low, top_value):
    def one(dim, parts):
        heights = jax.random.uniform(jax.random.fold_in(jax.random.fold_in(stream_key, 6), dim), (parts,), jnp.float32, low / len(pieces), top_value / len(pieces))
        return jnp.repeat(jnp.exp(heights), shape[dim] // parts).reshape((-1,) + (1,) * (len(shape) - dim - 1))

    loudness = one(*pieces[0])
    for cut in pieces[1:]:
        loudness = loudness * one(*cut)
    return loudness


def rank_table(amount, skew):
    portions = [(1 << 20) // math.isqrt(rank ** skew) + 1 for rank in range(1, amount + 1)]
    width = 1 + sum(portions) // (1 << 30)
    return np.cumsum(np.array([max(1, weight // width) for weight in portions]))


def skewed_ids(stream_key, extent, count, lean):
    listing = rank_table(count, lean)
    pick = jax.random.randint(jax.random.fold_in(stream_key, 1), extent, 0, int(listing[count - 1]))
    rank = jnp.searchsorted(jnp.asarray(listing, jnp.int32), pick, side="right")
    return jax.random.permutation(jax.random.fold_in(stream_key, 2), count)[rank].astype(jnp.int32)


def length_profile(number_of, total, most, skew):
    portions = [(1 << 20) // math.isqrt(rank ** skew) + 1 for rank in range(2, number_of + 1)]
    surplus, holding = total - most - (number_of - 1), [1] * (number_of - 1)
    while surplus > 0:
        free = [i for i in range(number_of - 1) if holding[i] < most]
        mass, budget = sum([portions[i] for i in free]), surplus
        for i in free:
            addition = min(most - holding[i], max(1, budget * portions[i] // mass), surplus)
            holding[i] = holding[i] + addition
            surplus = surplus - addition
    return np.array([most] + holding)


def ragged(key, count, total, reach, slope):
    if count == 2:
        one = jax.random.randint(key, (), max(1, total - reach), min(reach, total - 1) + 1)
        return jnp.stack([one, total - one])
    sizes = jnp.asarray(length_profile(count, total, reach, slope), jnp.int32)
    twos = (count - 1) // 2
    giver, receiver = sizes[1:1 + 2 * twos:2], sizes[2:2 + 2 * twos:2]
    slack = jnp.minimum(giver - 1, reach - receiver)
    shifted = jax.random.randint(jax.random.fold_in(key, 1), (twos,), 0, 1 << 20) % (slack + 1)
    sizes = sizes.at[1:1 + 2 * twos:2].set(giver - shifted).at[2:2 + 2 * twos:2].set(receiver + shifted)
    return sizes[jax.random.permutation(jax.random.fold_in(key, 2), count)]


def normal_values(rng, extent, deviation, reach, shards=(), held_as=jnp.bfloat16):
    values = deviation * jax.random.normal(rng, extent, jnp.float32)
    if shards:
        values = values * shard_levels(rng, extent, shards, -0.22, 0.18)
    return jnp.clip(values, -reach, reach).astype(held_as)


def setup_inputs(seed: int = 0) -> dict:
    arg_keys = jax.random.split(jax.random.key(seed), 13)
    tokens = draw_tokens(jax.random.fold_in(arg_keys[12], 71), 0)
    attend_weight = normal_values(arg_keys[1], (D, 3 * D), D ** -0.5, 0.1875)
    output_weight = normal_values(arg_keys[2], (D, D), D ** -0.5, 0.1875)
    attend_gain = jnp.clip(1.0 + 0.18 * jax.random.normal(arg_keys[3], (D,), jnp.float32), 0.1, 1.9)
    up_weight = normal_values(arg_keys[4], (D, FF), D ** -0.5, 0.1875, ((1, 8),))
    down_weight = normal_values(arg_keys[5], (D, FF), FF ** -0.5, 0.09375, ((1, 8),))
    mlp_gain = jnp.clip(1.0 + 0.18 * jax.random.normal(arg_keys[6], (D,), jnp.float32), 0.1, 1.9)
    embed_weight = normal_values(arg_keys[7], (D, P_SIZE), D ** -0.5, 0.1875)
    query_length = ragged(arg_keys[8], REQS, REQS * SEQ * 3 // 4, SEQ, 1).astype(jnp.int32)
    documents = draw_documents(jax.random.fold_in(arg_keys[12], 71), 0)
    document_length = ragged(arg_keys[10], DOCS, DOCS * DLEN // 2 + DOCS, DLEN, 1).astype(jnp.int32)
    candidates = touch_ends(skewed_ids(arg_keys[11], (REQS, CAND), DOCS, 2), jax.random.fold_in(arg_keys[11], 3), 0, DOCS - 1).astype(jnp.int32)
    return {"tokens": tokens, "attend_weight": attend_weight, "output_weight": output_weight, "attend_gain": attend_gain, "up_weight": up_weight, "down_weight": down_weight, "mlp_gain": mlp_gain, "embed_weight": embed_weight, "query_length": query_length, "documents": documents, "document_length": document_length, "candidates": candidates}


def norm_rows(values, scaling):
    average = lax.optimization_barrier(jnp.mean(values, axis=-1, keepdims=True))
    centred = values - average
    variance = lax.optimization_barrier(jnp.mean(centred * centred, axis=-1, keepdims=True))
    return centred * lax.rsqrt(variance + 1e-05) * scaling.astype(jnp.float32)

def reference(tokens, attend_weight, output_weight, attend_gain, up_weight, down_weight, mlp_gain, embed_weight, query_length, documents, document_length, candidates):
    rows = tokens.shape[0]
    requests = query_length.shape[0]
    packed = jnp.dot(tokens, attend_weight, preferred_element_type=jnp.float32).astype(jnp.bfloat16)
    packed = packed.reshape(requests, SEQ, 3, HEADS, HD).astype(jnp.float32)
    live_slot = jnp.arange(SEQ)[None, :] < query_length[:, None]
    logits = jnp.einsum('rqhd,rkhd->rhqk', packed[:, :, 0], packed[:, :, 1]) * HD ** (-0.5)
    logits = jnp.where(live_slot[:, None, None, :], logits, -1e+30)
    highest = lax.optimization_barrier(jnp.max(logits, axis=-1, keepdims=True))
    weights = jnp.exp(logits - highest)
    probs = (weights / lax.optimization_barrier(jnp.sum(weights, axis=-1, keepdims=True))).astype(jnp.bfloat16)
    context = jnp.einsum('rhqk,rkhd->rqhd', probs.astype(jnp.float32), packed[:, :, 2])
    context = context.astype(jnp.bfloat16).reshape(rows, D)
    attended = jnp.dot(context, output_weight, preferred_element_type=jnp.float32)
    normed = norm_rows(tokens.astype(jnp.float32) + attended, attend_gain).astype(jnp.bfloat16)
    inner = jax.nn.gelu(jnp.dot(normed, up_weight, preferred_element_type=jnp.float32), approximate=False).astype(jnp.bfloat16)
    reduced = jnp.dot(inner, down_weight.T, preferred_element_type=jnp.float32)
    layer_out = norm_rows(normed.astype(jnp.float32) + reduced, mlp_gain).astype(jnp.bfloat16)
    projected = jnp.dot(layer_out, embed_weight, preferred_element_type=jnp.float32)
    unit = projected * lax.rsqrt(lax.optimization_barrier(jnp.sum(projected * projected, axis=-1, keepdims=True)) + 1e-06)
    embedded = jnp.where(live_slot.reshape(rows, 1), unit, 0.0).astype(jnp.bfloat16)

    def score_one(item):
        block, picks = item
        chosen = documents[picks].astype(jnp.float32)
        limits = document_length[picks]
        sims = jnp.einsum('sp,ctp->sct', block.astype(jnp.float32), chosen)
        live_doc = jnp.arange(DLEN)[None, :] < limits[:, None]
        sims = jnp.where(live_doc[None], sims, -1e+30)
        return lax.optimization_barrier(jnp.sum(lax.optimization_barrier(jnp.max(sims, axis=2)), axis=0))
    scores = lax.map(score_one, (embedded.reshape(requests, SEQ, P_SIZE), candidates))
    return (embedded, scores)
```

```python
import functools

import jax
import jax.numpy as jnp
from jax import lax
from jax.experimental import pallas as pl
from jax.experimental.pallas import tpu as pltpu
from jax.sharding import PartitionSpec as P

D = 1024
HEADS = 16
HD = 64
P_SIZE = 128
SEQ = 128
LANES = 128
SLABS = 2 * D // LANES
DEAD = -1e30
VMEM_LIMIT = 56 * 1024 * 1024
f32 = jnp.float32
bf16 = jnp.bfloat16


def dot(a, b):
    return jnp.dot(a, b, preferred_element_type=f32)


def dot_t(a, b):
    return lax.dot_general(a, b, (((1,), (1,)), ((), ())), preferred_element_type=f32)


def norm_rows(values, scaling):
    average = jnp.mean(values, axis=-1, keepdims=True)
    centred = values - average
    variance = jnp.mean(centred * centred, axis=-1, keepdims=True)
    return centred * lax.rsqrt(variance + 1e-05) * scaling


def gelu(x):
    return 0.5 * x * (1.0 + lax.erf(x * (0.5 ** 0.5)))


def params(**kw):
    return pltpu.CompilerParams(vmem_limit_bytes=VMEM_LIMIT, **kw)


def vmem(n=1):
    return [pl.BlockSpec(memory_space=pltpu.VMEM)] * n


def pack_body(up, down, out):
    for j in range(SLABS // 2):
        rows = slice(j * LANES, (j + 1) * LANES)
        out[j] = up[rows, :].T
        out[SLABS // 2 + j] = down[rows, :].T


def attend_body(length, tok, qkv, wo, gain, out, packed, context):
    rows_all = tok.shape[0]
    for c in range(0, 3 * D, 512):
        packed[:, c : c + 512] = dot(tok[...], qkv[:, c : c + 512]).astype(bf16)
    lane = lax.broadcasted_iota(jnp.int32, (2 * SEQ, LANES), 1)
    low = lax.broadcasted_iota(jnp.int32, (SEQ, LANES), 1) < HD

    def request(r, carry):
        rows = pl.ds(pl.multiple_of(r * SEQ, SEQ), SEQ)
        live = lane < length[r]
        for p in range(HEADS // 2):
            at = p * LANES
            q = packed[rows, at : at + LANES]
            k = packed[rows, D + at : D + at + LANES]
            v = packed[rows, 2 * D + at : 2 * D + at + LANES]
            zero = jnp.zeros_like(q)
            both = jnp.concatenate([jnp.where(low, q, zero), jnp.where(low, zero, q)], axis=0)
            logits = jnp.where(live, dot_t(both, k) * HD ** (-0.5), DEAD)
            weights = jnp.exp(logits - jnp.max(logits, axis=-1, keepdims=True))
            probs = (weights * (1.0 / jnp.sum(weights, axis=-1, keepdims=True))).astype(bf16)
            ctx = dot(probs, v)
            context[rows, at : at + LANES] = jnp.where(low, ctx[:SEQ], ctx[SEQ:]).astype(bf16)
        return carry

    lax.fori_loop(0, rows_all // SEQ, request, 0)
    attended = dot(context[...], wo[...])
    out[...] = norm_rows(tok[...].astype(f32) + attended, gain[...]).astype(bf16)


def attend(tokens, qkv, wo, gain, length):
    rows = tokens.shape[0]
    return pl.pallas_call(
        attend_body,
        out_shape=jax.ShapeDtypeStruct((rows, D), bf16),
        in_specs=[pl.BlockSpec(memory_space=pltpu.SMEM)] + vmem(4),
        out_specs=vmem()[0],
        scratch_shapes=[pltpu.VMEM((rows, 3 * D), bf16), pltpu.VMEM((rows, D), bf16)],
        compiler_params=params(),
        name="attend",
    )(length, tokens, qkv, wo, gain.reshape(1, D))


def pack(up, down):
    return pl.pallas_call(
        pack_body,
        out_shape=jax.ShapeDtypeStruct((SLABS, up.shape[1], LANES), bf16),
        in_specs=vmem(2),
        out_specs=vmem()[0],
        compiler_params=params(),
        name="pack",
    )(up, down)


def ffn_body(length, normed, piece, gain, we, out, acc):
    step = pl.program_id(0)

    @pl.when(step == 0)
    def _():
        acc[...] = jnp.zeros_like(acc)

    n = piece.shape[2]
    half = SLABS // 2
    sub = 256
    x = normed[...]
    for s in range(0, n, sub):
        wu = jnp.concatenate([piece[0, j, s : s + sub] for j in range(half)], axis=1)
        wd = jnp.concatenate([piece[0, half + j, s : s + sub] for j in range(half)], axis=1)
        acc[...] += dot(gelu(dot_t(x, wu)).astype(bf16), wd)

    @pl.when(step == pl.num_programs(0) - 1)
    def _():
        layer = norm_rows(normed[...].astype(f32) + acc[...], gain[...]).astype(bf16)
        projected = dot(layer, we[...])
        unit = projected * lax.rsqrt(jnp.sum(projected * projected, axis=-1, keepdims=True) + 1e-06)
        slot = lax.broadcasted_iota(jnp.int32, (SEQ, P_SIZE), 0)
        for r in range(normed.shape[0] // SEQ):
            rows = slice(r * SEQ, (r + 1) * SEQ)
            out[rows, :] = jnp.where(slot < length[r], unit[rows], 0.0).astype(bf16)


def ffn(normed, pieces, gain, we, length):
    rows = normed.shape[0]
    return pl.pallas_call(
        ffn_body,
        grid=(pieces.shape[0],),
        out_shape=jax.ShapeDtypeStruct((rows, P_SIZE), bf16),
        in_specs=[
            pl.BlockSpec(memory_space=pltpu.SMEM),
            pl.BlockSpec((rows, D), lambda i: (0, 0)),
            pl.BlockSpec((1,) + pieces.shape[1:], lambda i: (i, 0, 0, 0)),
            pl.BlockSpec((1, D), lambda i: (0, 0)),
            pl.BlockSpec((D, P_SIZE), lambda i: (0, 0)),
        ],
        out_specs=pl.BlockSpec((rows, P_SIZE), lambda i: (0, 0)),
        scratch_shapes=[pltpu.VMEM((rows, D), f32)],
        compiler_params=params(),
        name="ffn",
    )(length, normed, pieces, gain.reshape(1, D), we)


def score_body(cand, emb, docs, out, held, lens, best, sem, lsem):
    groups, slices = docs.shape[0], docs.shape[1]
    picks = cand.shape[0]
    per = 8
    toks = 32

    def fetch(i):
        e = cand[i]
        return pltpu.make_async_copy(
            docs.at[e // per, :, pl.ds(pl.multiple_of((e % per) * toks, toks), toks), :], held.at[i], sem.at[i]
        )

    lencopy = pltpu.make_async_copy(docs.at[:, 0, pl.ds(per * toks, 16), :], lens, lsem)
    lencopy.start()
    for i in range(picks):
        fetch(i).start()
    lencopy.wait()
    pos = lax.broadcasted_iota(jnp.int32, (slices * toks, LANES), 0).astype(f32)
    row = lax.broadcasted_iota(jnp.int32, (16, LANES), 0)
    for i in range(picks):
        fetch(i).wait()
        e = cand[i]
        block = lens[e // per].astype(f32)
        limit = jnp.sum(jnp.where(row == e % per, block, 0.0), axis=0, keepdims=True)
        q = emb[(i // 8) * SEQ : (i // 8 + 1) * SEQ, :]
        sims = dot_t(held[i].reshape(slices * toks, P_SIZE), q)
        best[i // 8, pl.ds(i % 8, 1), :] = jnp.max(jnp.where(pos < limit, sims, DEAD), axis=0, keepdims=True)
    out[...] = jnp.sum(best[...], axis=-1)


def score(cand, emb, docs):
    requests, picks = cand.shape
    total = requests * picks
    return pl.pallas_call(
        score_body,
        out_shape=jax.ShapeDtypeStruct((requests, picks), f32),
        in_specs=[
            pl.BlockSpec(memory_space=pltpu.SMEM),
            pl.BlockSpec(memory_space=pltpu.VMEM),
            pl.BlockSpec(memory_space=pl.ANY),
        ],
        out_specs=vmem()[0],
        scratch_shapes=[
            pltpu.VMEM((total, 8, 32, P_SIZE), bf16),
            pltpu.VMEM((16, 16, LANES), bf16),
            pltpu.VMEM((requests, picks, LANES), f32),
            pltpu.SemaphoreType.DMA((total,)),
            pltpu.SemaphoreType.DMA(()),
        ],
        compiler_params=params(),
        name="score",
    )(cand.reshape(-1), emb, docs)


def on_device(
    tokens,
    attend_weight,
    output_weight,
    attend_gain,
    up_weight,
    down_weight,
    mlp_gain,
    embed_weight,
    query_length,
    documents,
    document_length,
    candidates,
):
    held = documents.shape[0]
    weights = pack(up_weight, down_weight)
    pieces = lax.all_gather(weights, "mlp", axis=0, tiled=False)
    limits = jnp.broadcast_to(document_length.astype(bf16)[:, None], (held, P_SIZE))
    block = jnp.concatenate(
        [documents.reshape(-1, P_SIZE), limits, jnp.zeros((16 - held, P_SIZE), bf16)], axis=0
    )
    docs = lax.all_gather(block, ("req", "mlp"), axis=0, tiled=False)
    docs = docs.reshape(16, 8, block.shape[0], P_SIZE)
    normed = attend(tokens, attend_weight, output_weight, attend_gain, query_length)
    embedded = ffn(normed, pieces, mlp_gain, embed_weight, query_length)
    scores = score(candidates, embedded, docs)
    return (embedded, scores)


def solution(mesh):
    return jax.shard_map(
        on_device,
        mesh=mesh,
        in_specs=(
            P(("req", "mlp"), None),
            P(),
            P(),
            P(),
            P(None, "mlp"),
            P(None, "mlp"),
            P(),
            P(),
            P(("req", "mlp")),
            P("req", "mlp", None),
            P("req"),
            P(("req", "mlp"), None),
        ),
        out_specs=(P(("req", "mlp"), None), P(("req", "mlp"), None)),
        check_vma=False,
    )
```

```python
import functools

import jax
import jax.numpy as jnp
from jax import lax
from jax.experimental import pallas as pl
from jax.experimental.pallas import tpu as pltpu
from jax.sharding import PartitionSpec as P

D = 1024
HEADS = 16
HD = 64
P_SIZE = 128
SEQ = 128
LANES = 128
SLABS = 2 * D // LANES
HALF = SLABS // 2
TOKS = 32
DOC_ROWS = 144
SLICE = 32
AROUND = (0, 3, 1, 2)
DEAD = -1e30
f32 = jnp.float32
bf16 = jnp.bfloat16


def dot(a, b):
    return jnp.dot(a, b, preferred_element_type=f32)


def dot_t(a, b):
    return lax.dot_general(a, b, (((1,), (1,)), ((), ())), preferred_element_type=f32)


def norm_rows(values, scaling):
    average = jnp.mean(values, axis=-1, keepdims=True)
    centred = values - average
    variance = jnp.mean(centred * centred, axis=-1, keepdims=True)
    return centred * lax.rsqrt(variance + 1e-05) * scaling


def gelu(x):
    return 0.5 * x * (1.0 + lax.erf(x * (0.5 ** 0.5)))


def params(mib):
    return pltpu.CompilerParams(vmem_limit_bytes=mib * 1024 * 1024)


def vmem(n=1):
    return [pl.BlockSpec(memory_space=pltpu.VMEM)] * n


def place(z, x, y, c):
    return ((z % 4) * 4 + x % 4) * 8 + (y % 4) * 2 + c % 2


def shift(dz=0, dx=0, dy=0, dc=0):
    return [
        (place(z, x, y, c), place(z + dz, x + dx, y + dy, c + dc))
        for z in range(4)
        for x in range(4)
        for y in range(4)
        for c in range(2)
    ]


STEPS = {
    "y+": shift(dy=1),
    "y-": shift(dy=-1),
    "y2": shift(dy=2),
    "x+": shift(dx=1),
    "x-": shift(dx=-1),
    "x2": shift(dx=2),
    "z+": shift(dz=1),
    "z-": shift(dz=-1),
    "z2": shift(dz=2),
    "c": shift(dc=1),
}


def send(value, way):
    return lax.ppermute(value, ("req", "mlp"), STEPS[way])


def after(value, *first):
    return lax.optimization_barrier((value, first))[0]


def first_body(where, up, down, docs, limits, out, turned):
    for part in range(2):
        lanes = slice(256 + part * LANES, 256 + (part + 1) * LANES)
        start = pl.multiple_of(where[1 - part] * SLICE, SLICE)
        for j in range(HALF):
            rows = slice(j * LANES, (j + 1) * LANES)
            for k, w in ((j, up), (HALF + j, down)):
                turned[...] = w[rows, lanes].T
                at = k * 2 * SLICE + part * SLICE
                out[at : at + SLICE, :] = turned[pl.ds(start, SLICE), :]
    base = SLABS * 2 * SLICE
    for h in range(2):
        at = base + h * DOC_ROWS
        out[at : at + 4 * TOKS, :] = docs[h * 4 * TOKS : (h + 1) * 4 * TOKS, :]
        row = lax.broadcasted_iota(jnp.int32, (16, LANES), 0)
        limit = jnp.zeros((16, LANES), f32)
        for j in range(4):
            limit = jnp.where(row == j, limits[h * 4 + j].astype(f32), limit)
        out[at + 4 * TOKS : at + DOC_ROWS, :] = limit.astype(bf16)


def first(where, up, down, docs, limits):
    smem = pl.BlockSpec(memory_space=pltpu.SMEM)
    return pl.pallas_call(
        first_body,
        out_shape=jax.ShapeDtypeStruct((SLABS * 2 * SLICE + 2 * DOC_ROWS, LANES), bf16),
        in_specs=[smem] + vmem(3) + [smem],
        out_specs=vmem()[0],
        scratch_shapes=[pltpu.VMEM((LANES, LANES), bf16)],
        compiler_params=params(16),
        name="first",
    )(where, up, down, docs, limits)


def pack_body(up, down, low, high):
    for j in range(HALF):
        rows = slice(j * LANES, (j + 1) * LANES)
        low[j] = up[rows, :256].T
        low[HALF + j] = down[rows, :256].T
        high[j] = up[rows, 256:].T
        high[HALF + j] = down[rows, 256:].T


def pack(up, down):
    piece = jax.ShapeDtypeStruct((SLABS, 256, LANES), bf16)
    return pl.pallas_call(
        pack_body,
        out_shape=(piece, piece),
        in_specs=vmem(2),
        out_specs=tuple(vmem(2)),
        compiler_params=params(16),
        name="pack",
    )(up, down)


def units(refs, half, start, size):
    slabs = []
    for j in range(HALF):
        parts, at = [], 0
        for ref, count in refs:
            low, high = max(start, at), min(start + size, at + count)
            if low < high:
                parts.append(ref[half * HALF + j, low - at : high - at])
            at += count
        slabs.append(parts[0] if len(parts) == 1 else jnp.concatenate(parts, axis=0))
    return jnp.concatenate(slabs, axis=1)


def attend_body(length, tok, qkv, wo, gain, out, packed, context):
    rows_all = tok.shape[0]
    for c in range(0, 3 * D, 512):
        packed[:, c : c + 512] = dot(tok[...], qkv[:, c : c + 512]).astype(bf16)
    lane = lax.broadcasted_iota(jnp.int32, (2 * SEQ, LANES), 1)
    low = lax.broadcasted_iota(jnp.int32, (SEQ, LANES), 1) < HD

    def request(r, carry):
        rows = pl.ds(pl.multiple_of(r * SEQ, SEQ), SEQ)
        live = lane < length[r]
        for p in range(HEADS // 2):
            at = p * LANES
            q = packed[rows, at : at + LANES]
            k = packed[rows, D + at : D + at + LANES]
            v = packed[rows, 2 * D + at : 2 * D + at + LANES]
            zero = jnp.zeros_like(q)
            both = jnp.concatenate([jnp.where(low, q, zero), jnp.where(low, zero, q)], axis=0)
            logits = jnp.where(live, dot_t(both, k) * HD ** (-0.5), DEAD)
            weights = jnp.exp(logits - jnp.max(logits, axis=-1, keepdims=True))
            probs = (weights * (1.0 / jnp.sum(weights, axis=-1, keepdims=True))).astype(bf16)
            ctx = dot(probs, v)
            context[rows, at : at + LANES] = jnp.where(low, ctx[:SEQ], ctx[SEQ:]).astype(bf16)
        return carry

    lax.fori_loop(0, rows_all // SEQ, request, 0)
    attended = dot(context[...], wo[...])
    out[...] = norm_rows(tok[...].astype(f32) + attended, gain[...]).astype(bf16)


def attend(tokens, qkv, wo, gain, length):
    rows = tokens.shape[0]
    return pl.pallas_call(
        attend_body,
        out_shape=jax.ShapeDtypeStruct((rows, D), bf16),
        in_specs=[pl.BlockSpec(memory_space=pltpu.SMEM)] + vmem(4),
        out_specs=vmem()[0],
        scratch_shapes=[pltpu.VMEM((rows, 3 * D), bf16), pltpu.VMEM((rows, D), bf16)],
        compiler_params=params(32),
        cost_estimate=pl.CostEstimate(flops=8 * rows * D * D, transcendentals=0, bytes_accessed=8 * D * D),
        name="attend",
    )(length, tokens, qkv, wo, gain.reshape(1, D))


def ffn_body(counts, sub, fresh, *refs):
    tokens = refs[0]
    old = None if fresh else refs[1]
    pieces = list(zip(refs[1 if fresh else 2 : -1], counts))
    out = refs[-1]
    total = sum(counts)
    x = tokens[...]
    acc = None if fresh else old[...]
    for s in range(0, total, sub):
        n = min(sub, total - s)
        inner = gelu(dot_t(x, units(pieces, 0, s, n))).astype(bf16)
        more = dot(inner, units(pieces, 1, s, n))
        acc = more if acc is None else acc + more
    out[...] = acc


def ffn(tokens, old, pieces, name, sub=256):
    rows = tokens.shape[0]
    counts = tuple(p.shape[1] for p in pieces)
    tail = ((tokens,) if old is None else (tokens, old)) + tuple(pieces)
    return pl.pallas_call(
        functools.partial(ffn_body, counts, sub, old is None),
        out_shape=jax.ShapeDtypeStruct((rows, D), f32),
        in_specs=vmem(len(tail)),
        out_specs=vmem()[0],
        input_output_aliases={} if old is None else {1: 0},
        compiler_params=params(32),
        cost_estimate=pl.CostEstimate(flops=4 * rows * D * sum(counts), transcendentals=0, bytes_accessed=4 * D * sum(counts)),
        name=name,
    )(*tail)


def embed_body(length, normed, mine, other, gain, we, out):
    layer = norm_rows(normed[...].astype(f32) + (mine[...] + other[...]), gain[...]).astype(bf16)
    projected = dot(layer, we[...])
    unit = projected * lax.rsqrt(jnp.sum(projected * projected, axis=-1, keepdims=True) + 1e-06)
    slot = lax.broadcasted_iota(jnp.int32, (SEQ, P_SIZE), 0)
    for r in range(normed.shape[0] // SEQ):
        rows = slice(r * SEQ, (r + 1) * SEQ)
        out[rows, :] = jnp.where(slot < length[r], unit[rows], 0.0).astype(bf16)


def embed(length, normed, mine, other, gain, we):
    return pl.pallas_call(
        embed_body,
        out_shape=jax.ShapeDtypeStruct((normed.shape[0], P_SIZE), bf16),
        in_specs=[pl.BlockSpec(memory_space=pltpu.SMEM)] + vmem(5),
        out_specs=vmem()[0],
        compiler_params=params(24),
        name="embed",
    )(length, normed, mine, other, gain.reshape(1, D), we)


def score_body(where, cand, pair, emb, sib, *refs):
    docs, out, held, sem = refs[:8], refs[8], refs[9], refs[10]
    copies = [pltpu.make_async_copy(docs[i], held.at[i], sem.at[i]) for i in range(8)]
    for copy in copies:
        copy.start()
    z, x, y, c = where[0], where[1], where[2], where[3]
    local = lax.broadcasted_iota(jnp.int32, (TOKS, LANES), 0)
    pos = jnp.concatenate(
        [local + TOKS * (2 * ((y + d) & 3) + c) for d in AROUND], axis=0
    ).astype(f32)
    row = lax.broadcasted_iota(jnp.int32, (16, LANES), 0)

    def slot(d):
        return jnp.where(d == 0, 0, jnp.where(d == 3, 1, d + 1))

    for copy in copies:
        copy.wait()
    per = cand.shape[0]
    for i in range(2 * per):
        e = cand[i] if i < per else pair[i - per]
        tokens = emb if i < per else sib
        j, req = e & 7, e >> 3
        sz, sx = slot(((req >> 2) - z) & 3), slot(((req & 3) - x) & 3)
        h, j4 = j >> 2, j & 3
        outer = h * 4 + jnp.where(h == 0, sz, sx)
        within = jnp.where(h == 0, sx, sz)
        block = held[outer, within, :, pl.ds(pl.multiple_of(j4 * TOKS, TOKS), TOKS), :]
        lens = held[outer, within, 0, 4 * TOKS : DOC_ROWS, :].astype(f32)
        limit = jnp.sum(jnp.where(row == j4, lens, 0.0), axis=0, keepdims=True)
        r = (i % per) // 8
        sims = dot_t(block.reshape(4 * TOKS, P_SIZE), tokens[r * SEQ : (r + 1) * SEQ, :])
        out[i : i + 1, :] = jnp.max(jnp.where(pos < limit, sims, DEAD), axis=0, keepdims=True)


def score(where, cand, pair, emb, sib, docs):
    smem = pl.BlockSpec(memory_space=pltpu.SMEM)
    total = 2 * cand.size
    docs = [d.reshape(4, 4, DOC_ROWS, P_SIZE) for d in docs]
    return pl.pallas_call(
        score_body,
        out_shape=jax.ShapeDtypeStruct((total, SEQ), f32),
        in_specs=[smem] * 3 + vmem(2) + [pl.BlockSpec(memory_space=pl.ANY)] * 8,
        out_specs=vmem()[0],
        scratch_shapes=[
            pltpu.VMEM((8, 4, 4, DOC_ROWS, P_SIZE), bf16),
            pltpu.SemaphoreType.DMA((8,)),
        ],
        compiler_params=params(16),
        name="score",
    )(where, cand.reshape(-1), pair.reshape(-1), emb, sib, *docs)


def on_device(
    tokens,
    attend_weight,
    output_weight,
    attend_gain,
    up_weight,
    down_weight,
    mlp_gain,
    embed_weight,
    query_length,
    documents,
    document_length,
    candidates,
):
    req, mlp = lax.axis_index("req"), lax.axis_index("mlp")
    where = jnp.stack([req // 4, req % 4, mlp // 2, mlp % 2]).astype(jnp.int32)
    pair = send(candidates, "c")
    start = first(where, up_weight, down_weight, documents.reshape(-1, P_SIZE), document_length)
    near = [send(start, way) for way in ("y+", "y-", "y2")]
    low, high = pack(up_weight, down_weight)
    normed = attend(tokens, attend_weight, output_weight, attend_gain, query_length)
    pair_normed = send(normed, "c")
    both = jnp.concatenate([normed, pair_normed], axis=0)

    size = SLABS * 2 * SLICE
    slices = [n[:size].reshape(SLABS, 2 * SLICE, LANES) for n in near]
    blocks = [start] + near
    halves = [[b[size + h * DOC_ROWS : size + (h + 1) * DOC_ROWS] for b in blocks] for h in range(2)]
    flat = SLABS * 3 * SLICE
    go = [
        jnp.concatenate(
            [jnp.concatenate([s[:, h * SLICE : (h + 1) * SLICE] for s in slices], axis=1).reshape(flat, LANES)]
            + halves[h],
            axis=0,
        )
        for h in range(2)
    ]
    axes = ("x", "z")
    came = [[send(go[h], axes[h] + way) for way in ("+", "-")] for h in range(2)]
    low_go = after(low, *near)
    low_far = send(low_go, "y2")
    for h in range(2):
        came[h].append(send(go[h], axes[h] + "2"))
    low_go = after(low, *came[0][:2], *came[1][:2])
    low_near = [send(low_go, "y+"), send(low_go, "y-")]
    wide = [[a[:flat].reshape(SLABS, 3 * SLICE, LANES) for a in came[h]] for h in range(2)]
    total = ffn(both, None, [low, high], "ffn1")
    total = ffn(both, total, slices + wide[0][:2] + wide[1][:2], "ffn2")
    docs = [jnp.concatenate([go[h][flat:]] + [a[flat:] for a in came[h]], axis=0) for h in range(2)]
    last = [[send(docs[h], axes[1 - h] + way) for way in ("+", "-", "2")] for h in range(2)]
    total = ffn(both, total, [wide[0][2], wide[1][2], low_far], "ffn3")
    rows = normed.shape[0]
    away = ffn(pair_normed, total[rows:], low_near, "ffn4")
    other = send(away, "c")
    mine = ffn(normed, total[:rows], low_near, "ffn5")
    embedded = embed(query_length, normed, mine, other, mlp_gain, embed_weight)
    sib = send(embedded, "c")
    best = score(where, candidates, pair, embedded, sib, [docs[0]] + last[0] + [docs[1]] + last[1])
    half = best.shape[0] // 2
    best = jnp.maximum(best[:half], send(best[half:], "c"))
    scores = jnp.sum(best, axis=1).reshape(candidates.shape)
    return (embedded, scores)


def solution(mesh):
    return jax.shard_map(
        on_device,
        mesh=mesh,
        in_specs=(
            P(("req", "mlp"), None),
            P(),
            P(),
            P(),
            P(None, "mlp"),
            P(None, "mlp"),
            P(),
            P(),
            P(("req", "mlp")),
            P("req", "mlp", None),
            P("req"),
            P(("req", "mlp"), None),
        ),
        out_specs=(P(("req", "mlp"), None), P(("req", "mlp"), None)),
        check_vma=False,
    )
```

```python
import functools

import jax
import jax.numpy as jnp
from jax import lax
from jax.experimental import pallas as pl
from jax.experimental.pallas import tpu as pltpu
from jax.sharding import PartitionSpec as P

D = 1024
HEADS = 16
HD = 64
P_SIZE = 128
SEQ = 128
LANES = 128
SLABS = 2 * D // LANES
HALF = SLABS // 2
TOKS = 32
DOC_ROWS = 272
SLICE = 64
PART = SLABS * SLICE
BLOCK = PART + DOC_ROWS
AROUND = (0, 3, 1, 2)
AROUND_Y = (3, 1, 2, 0)
DEAD = -1e30
f32 = jnp.float32
bf16 = jnp.bfloat16


def dot(a, b):
    return jnp.dot(a, b, preferred_element_type=f32)


def dot_t(a, b):
    return lax.dot_general(a, b, (((1,), (1,)), ((), ())), preferred_element_type=f32)


def norm_rows(values, scaling):
    average = jnp.mean(values, axis=-1, keepdims=True)
    centred = values - average
    variance = jnp.mean(centred * centred, axis=-1, keepdims=True)
    return centred * lax.rsqrt(variance + 1e-05) * scaling


def gelu(x):
    return 0.5 * x * (1.0 + lax.erf(x * (0.5 ** 0.5)))


LIGHT = pl.CostEstimate(flops=1, transcendentals=0, bytes_accessed=1)


def params(mib):
    return pltpu.CompilerParams(vmem_limit_bytes=mib * 1024 * 1024)


def vmem(n=1):
    return [pl.BlockSpec(memory_space=pltpu.VMEM)] * n


def place(z, x, y, c):
    return ((z % 4) * 4 + x % 4) * 8 + (y % 4) * 2 + c % 2


def shift(move):
    return [
        (place(z, x, y, c), place(*move(z, x, y, c)))
        for z in range(4)
        for x in range(4)
        for y in range(4)
        for c in range(2)
    ]


def along_y(d):
    return shift(lambda z, x, y, c: (z, x, y + d, c))


def crossed(d, first):
    return shift(lambda z, x, y, c: (z, x + d, y, c) if c == first else (z + d, x, y, c))


STEPS = {"y+": along_y(1), "y-": along_y(-1), "y2": along_y(2)}
for name, d in (("+", 1), ("-", -1), ("2", 2)):
    STEPS["f" + name] = crossed(d, 0)
    STEPS["g" + name] = crossed(d, 1)
STEPS["c"] = shift(lambda z, x, y, c: (z, x, y, c + 1))


def send(value, way):
    return lax.ppermute(value, ("req", "mlp"), STEPS[way])


def after(value, *first):
    return lax.optimization_barrier((value, first))[0]


def any_spec(n=1):
    return [pl.BlockSpec(memory_space=pl.ANY)] * n


SMEM = pl.BlockSpec(memory_space=pltpu.SMEM)


def first_body(where, limits, up, down, docs, out, held, turned, sems):
    index = where[4]
    lanes = pl.ds(pl.multiple_of(256 + (index >> 1) * LANES, LANES), LANES)
    copies = [pltpu.make_async_copy(w.at[:, lanes], held.at[k], sems.at[k]) for k, w in enumerate((up, down))]
    tokens = DOC_ROWS - 16
    copies.append(pltpu.make_async_copy(docs, out.at[PART : PART + tokens], sems.at[2]))
    for copy in copies:
        copy.start()
    row = lax.broadcasted_iota(jnp.int32, (16, LANES), 0)
    limit = jnp.zeros((16, LANES), f32)
    for j in range(8):
        limit = jnp.where(row == j, limits[j].astype(f32), limit)
    out[PART + tokens : BLOCK, :] = limit.astype(bf16)
    start = pl.multiple_of((index & 1) * SLICE, SLICE)
    for k in range(2):
        copies[k].wait()
        for j in range(HALF):
            slab = k * HALF + j
            turned[slab] = held[k, j * LANES : (j + 1) * LANES, :].T
            out[slab * SLICE : (slab + 1) * SLICE, :] = turned[slab, pl.ds(start, SLICE), :]
    copies[2].wait()


def first(where, up, down, docs, limits):
    return pl.pallas_call(
        first_body,
        out_shape=jax.ShapeDtypeStruct((BLOCK, LANES), bf16),
        in_specs=[SMEM] * 2 + any_spec(3),
        out_specs=vmem()[0],
        scratch_shapes=[
            pltpu.VMEM((2, D, LANES), bf16),
            pltpu.VMEM((SLABS, LANES, LANES), bf16),
            pltpu.SemaphoreType.DMA((3,)),
        ],
        compiler_params=params(16),
        cost_estimate=LIGHT,
        name="first",
    )(where, limits, up, down, docs)


def pack_body(up, down, low, high):
    for j in range(HALF):
        rows = slice(j * LANES, (j + 1) * LANES)
        low[j] = up[rows, :256].T
        low[HALF + j] = down[rows, :256].T
        high[j] = up[rows, 256:].T
        high[HALF + j] = down[rows, 256:].T


def pack(up, down):
    piece = jax.ShapeDtypeStruct((SLABS, 256, LANES), bf16)
    low, high = pl.pallas_call(
        pack_body,
        out_shape=(piece, piece),
        in_specs=vmem(2),
        out_specs=tuple(vmem(2)),
        compiler_params=params(16),
        cost_estimate=LIGHT,
        name="pack",
    )(up, down)
    return low.reshape(-1, LANES), high.reshape(-1, LANES)


def join_body(takes, *refs):
    out, at = refs[-1], 0
    for k, start, size in takes:
        out[at : at + size, :] = refs[k][start : start + size, :]
        at += size


def join(arrays, takes, name):
    return pl.pallas_call(
        functools.partial(join_body, takes),
        out_shape=jax.ShapeDtypeStruct((sum(t[2] for t in takes), LANES), bf16),
        in_specs=vmem(len(arrays)),
        out_specs=vmem()[0],
        compiler_params=params(16),
        cost_estimate=LIGHT,
        name=name,
    )(*arrays)


def attend_body(length, tok, qkv, wo, gain, out, packed, context):
    rows_all = tok.shape[0]
    for c in range(0, 3 * D, 512):
        packed[:, c : c + 512] = dot(tok[...], qkv[:, c : c + 512]).astype(bf16)
    lane = lax.broadcasted_iota(jnp.int32, (2 * SEQ, LANES), 1)
    low = lax.broadcasted_iota(jnp.int32, (SEQ, LANES), 1) < HD

    def request(r, carry):
        rows = pl.ds(pl.multiple_of(r * SEQ, SEQ), SEQ)
        live = lane < length[r]
        for p in range(HEADS // 2):
            at = p * LANES
            q = packed[rows, at : at + LANES]
            k = packed[rows, D + at : D + at + LANES]
            v = packed[rows, 2 * D + at : 2 * D + at + LANES]
            zero = jnp.zeros_like(q)
            both = jnp.concatenate([jnp.where(low, q, zero), jnp.where(low, zero, q)], axis=0)
            logits = jnp.where(live, dot_t(both, k) * HD ** (-0.5), DEAD)
            weights = jnp.exp(logits - jnp.max(logits, axis=-1, keepdims=True))
            probs = (weights * (1.0 / jnp.sum(weights, axis=-1, keepdims=True))).astype(bf16)
            ctx = dot(probs, v)
            context[rows, at : at + LANES] = jnp.where(low, ctx[:SEQ], ctx[SEQ:]).astype(bf16)
        return carry

    lax.fori_loop(0, rows_all // SEQ, request, 0)
    attended = dot(context[...], wo[...])
    out[...] = norm_rows(tok[...].astype(f32) + attended, gain[...]).astype(bf16)


def attend(tokens, qkv, wo, gain, length):
    rows = tokens.shape[0]
    return pl.pallas_call(
        attend_body,
        out_shape=jax.ShapeDtypeStruct((rows, D), bf16),
        in_specs=[pl.BlockSpec(memory_space=pltpu.SMEM)] + vmem(4),
        out_specs=vmem()[0],
        scratch_shapes=[pltpu.VMEM((rows, 3 * D), bf16), pltpu.VMEM((rows, D), bf16)],
        compiler_params=params(32),
        cost_estimate=LIGHT,
        name="attend",
    )(length, tokens, qkv, wo, gain.reshape(1, D))


def units(refs, half, start, size):
    slabs = []
    for j in range(HALF):
        parts, at = [], 0
        for ref, base, count in refs:
            low, high = max(start, at), min(start + size, at + count)
            if low < high:
                row = base + (half * HALF + j) * count
                parts.append(ref[row + low - at : row + high - at, :])
            at += count
        slabs.append(parts[0] if len(parts) == 1 else jnp.concatenate(parts, axis=0))
    return jnp.concatenate(slabs, axis=1)


def ffn_body(pieces, arrays, fresh, *refs):
    tokens, out = refs[0], refs[-1]
    held = refs[-1 - arrays : -1]
    laid = [(held[k], base, count) for k, base, count in pieces]
    total = sum(count for _, _, count in pieces)
    x = tokens[...]
    acc = None if fresh else refs[1][...]
    for s in range(0, total, 256):
        n = min(256, total - s)
        inner = gelu(dot_t(x, units(laid, 0, s, n))).astype(bf16)
        more = dot(inner, units(laid, 1, s, n))
        acc = more if acc is None else acc + more
    out[...] = acc


def ffn(tokens, old, arrays, pieces, name):
    rows = tokens.shape[0]
    tail = ((tokens,) if old is None else (tokens, old)) + tuple(arrays)
    return pl.pallas_call(
        functools.partial(ffn_body, tuple(pieces), len(arrays), old is None),
        out_shape=jax.ShapeDtypeStruct((rows, D), f32),
        in_specs=vmem(len(tail)),
        out_specs=vmem()[0],
        input_output_aliases={} if old is None else {1: 0},
        compiler_params=params(32),
        cost_estimate=LIGHT,
        name=name,
    )(*tail)


def embed_body(length, normed, mine, other, gain, we, out):
    layer = norm_rows(normed[...].astype(f32) + (mine[...] + other[...]), gain[...]).astype(bf16)
    projected = dot(layer, we[...])
    unit = projected * lax.rsqrt(jnp.sum(projected * projected, axis=-1, keepdims=True) + 1e-06)
    slot = lax.broadcasted_iota(jnp.int32, (SEQ, P_SIZE), 0)
    for r in range(normed.shape[0] // SEQ):
        rows = slice(r * SEQ, (r + 1) * SEQ)
        out[rows, :] = jnp.where(slot < length[r], unit[rows], 0.0).astype(bf16)


def embed(length, normed, mine, other, gain, we):
    return pl.pallas_call(
        embed_body,
        out_shape=jax.ShapeDtypeStruct((normed.shape[0], P_SIZE), bf16),
        in_specs=[pl.BlockSpec(memory_space=pltpu.SMEM)] + vmem(5),
        out_specs=vmem()[0],
        compiler_params=params(24),
        cost_estimate=LIGHT,
        name="embed",
    )(length, normed, mine, other, gain.reshape(1, D), we)


def score_body(where, cand, pair, emb, sib, *refs):
    docs, out, held, sem = refs[:5], refs[5], refs[6], refs[7]
    copies = [pltpu.make_async_copy(docs[i], held.at[i], sem.at[i]) for i in range(3)]
    copies += [
        pltpu.make_async_copy(docs[3 + i], held.at[3, 2 * i : 2 * i + 2], sem.at[3 + i]) for i in range(2)
    ]
    for copy in copies:
        copy.start()
    z, x, y, c = where[0], where[1], where[2], where[3]
    local = lax.broadcasted_iota(jnp.int32, (TOKS, LANES), 0)
    pos = jnp.concatenate(
        [local + TOKS * (2 * ((y + d) & 3) + c) for d in AROUND_Y], axis=0
    ).astype(f32)
    row = lax.broadcasted_iota(jnp.int32, (16, LANES), 0)

    def slot(d):
        return jnp.where(d == 0, 0, jnp.where(d == 3, 1, d + 1))

    for copy in copies:
        copy.wait()
    per = cand.shape[0]
    for i in range(2 * per):
        e = cand[i] if i < per else pair[i - per]
        tokens = emb if i < per else sib
        j, req = e & 7, e >> 3
        sz, sx = slot(((req >> 2) - z) & 3), slot(((req & 3) - x) & 3)
        outer = jnp.where(c == 0, sz, sx)
        within = jnp.where(c == 0, sx, sz)
        block = held[outer, within, :, pl.ds(pl.multiple_of(j * TOKS, TOKS), TOKS), :]
        lens = held[outer, within, 0, 8 * TOKS : DOC_ROWS, :].astype(f32)
        limit = jnp.sum(jnp.where(row == j, lens, 0.0), axis=0, keepdims=True)
        r = (i % per) // 8
        sims = dot_t(block.reshape(4 * TOKS, P_SIZE), tokens[r * SEQ : (r + 1) * SEQ, :])
        out[i : i + 1, :] = jnp.max(jnp.where(pos < limit, sims, DEAD), axis=0, keepdims=True)


def score(where, cand, pair, emb, sib, docs):
    total = 2 * cand.size
    docs = [d.reshape(-1, 4, DOC_ROWS, P_SIZE) for d in docs]
    return pl.pallas_call(
        score_body,
        out_shape=jax.ShapeDtypeStruct((total, SEQ), f32),
        in_specs=[SMEM] * 3 + vmem(2) + any_spec(5),
        out_specs=vmem()[0],
        scratch_shapes=[
            pltpu.VMEM((4, 4, 4, DOC_ROWS, P_SIZE), bf16),
            pltpu.SemaphoreType.DMA((5,)),
        ],
        compiler_params=params(16),
        cost_estimate=LIGHT,
        name="score",
    )(where, cand.reshape(-1), pair.reshape(-1), emb, sib, *docs)


def on_device(
    tokens,
    attend_weight,
    output_weight,
    attend_gain,
    up_weight,
    down_weight,
    mlp_gain,
    embed_weight,
    query_length,
    documents,
    document_length,
    candidates,
):
    req, mlp = lax.axis_index("req"), lax.axis_index("mlp")
    z, x, y, c = req // 4, req % 4, mlp // 2, mlp % 2
    where = jnp.stack([z, x, y, c, jnp.where(c == 0, x, z)]).astype(jnp.int32)
    start = first(where, up_weight, down_weight, documents.reshape(-1, P_SIZE), document_length)
    near = [send(start, way) for way in ("y+", "y-", "y2")]
    low, high = pack(up_weight, down_weight)
    normed = attend(after(tokens, start), attend_weight, output_weight, attend_gain, query_length)
    near = after(tuple(near), normed, high)

    whole = [(k, 0, BLOCK) for k in range(3)] + [(3, PART, DOC_ROWS)]
    go = join([*near, start], whole, "join1")
    came = [send(go, way) for way in ("f+", "f-", "f2")]
    low_go = after(low, go)
    low_near = [send(low_go, "y+"), send(low_go, "y-")]
    parts = [(k, i * BLOCK, SLICE) for k in range(3) for i in range(3)]
    takes = [(k, at, DOC_ROWS) for k in range(4) for at in [i * BLOCK + PART for i in range(3)] + [3 * BLOCK]]
    docs = join([go, *came], takes, "join2")
    last = [send(docs, way) for way in ("g+", "g-")]
    pair_normed = send(after(normed, docs), "c")
    both = jnp.concatenate([normed, pair_normed], axis=0)
    low_near = after(tuple(low_near), docs)
    mid = 128
    ahead = join([low_near[0]], [(0, k * 256, mid) for k in range(SLABS)], "join3")
    behind = join([low_near[1]], [(0, k * 256 + mid, mid) for k in range(SLABS)], "join4")
    low_far = [send(ahead, "y+"), send(behind, "y-")]
    total = ffn(both, None, [low, high], [(0, 0, 256), (1, 0, 256)], "ffn1")
    total = ffn(both, total, tuple(near) + tuple(came), [(k, 0, SLICE) for k in range(3)] + [(k + 3, b, n) for k, b, n in parts], "ffn2")
    total = ffn(both, total, low_near, [(0, 0, 256), (1, 0, 256)], "ffn3")
    cut = docs.shape[0] // 2
    low_far = after(tuple(low_far), *last)
    last += [send(last[0][:cut], "g+"), send(last[1][cut:], "g-")]
    rows = normed.shape[0]
    rest = [(0, 0, mid), (1, 0, mid)]
    away = ffn(pair_normed, total[rows:], low_far, rest, "ffn4")
    other = send(away, "c")
    mine = ffn(normed, total[:rows], low_far, rest, "ffn5")
    embedded = embed(query_length, normed, mine, other, mlp_gain, embed_weight)
    sib = send(embedded, "c")
    pair = send(after(candidates, total), "c")
    best = score(where, candidates, pair, embedded, sib, [docs] + last)
    half = best.shape[0] // 2
    best = jnp.maximum(best[:half], send(best[half:], "c"))
    scores = jnp.sum(best, axis=1).reshape(candidates.shape)
    return (embedded, scores)


def solution(mesh):
    return jax.shard_map(
        on_device,
        mesh=mesh,
        in_specs=(
            P(("req", "mlp"), None),
            P(),
            P(),
            P(),
            P(None, "mlp"),
            P(None, "mlp"),
            P(),
            P(),
            P(("req", "mlp")),
            P("req", "mlp", None),
            P("req"),
            P(("req", "mlp"), None),
        ),
        out_specs=(P(("req", "mlp"), None), P(("req", "mlp"), None)),
        check_vma=False,
    )
```

```python
import functools

import jax
import jax.numpy as jnp
from jax import lax
from jax.experimental import pallas as pl
from jax.experimental.pallas import tpu as pltpu
from jax.sharding import PartitionSpec as P

D = 1024
HEADS = 16
HD = 64
P_SIZE = 128
SEQ = 128
LANES = 128
SLABS = 2 * D // LANES
HALF = SLABS // 2
TOKS = 32
DOC_ROWS = 272
SLICE = 64
PART = SLABS * SLICE
BLOCK = PART + DOC_ROWS
AROUND = (0, 3, 1, 2)
AROUND_Y = (3, 1, 2, 0)
DEAD = -1e30
f32 = jnp.float32
bf16 = jnp.bfloat16


def dot(a, b):
    return jnp.dot(a, b, preferred_element_type=f32)


def dot_t(a, b):
    return lax.dot_general(a, b, (((1,), (1,)), ((), ())), preferred_element_type=f32)


def norm_rows(values, scaling):
    average = jnp.mean(values, axis=-1, keepdims=True)
    centred = values - average
    variance = jnp.mean(centred * centred, axis=-1, keepdims=True)
    return centred * lax.rsqrt(variance + 1e-05) * scaling


def gelu(x):
    return 0.5 * x * (1.0 + lax.erf(x * (0.5 ** 0.5)))


LIGHT = pl.CostEstimate(flops=1, transcendentals=0, bytes_accessed=1)


def params(mib):
    return pltpu.CompilerParams(vmem_limit_bytes=mib * 1024 * 1024)


def vmem(n=1):
    return [pl.BlockSpec(memory_space=pltpu.VMEM)] * n


def place(z, x, y, c):
    return ((z % 4) * 4 + x % 4) * 8 + (y % 4) * 2 + c % 2


def shift(move):
    return [
        (place(z, x, y, c), place(*move(z, x, y, c)))
        for z in range(4)
        for x in range(4)
        for y in range(4)
        for c in range(2)
    ]


def along_y(d):
    return shift(lambda z, x, y, c: (z, x, y + d, c))


def crossed(d, first):
    return shift(lambda z, x, y, c: (z, x + d, y, c) if c == first else (z + d, x, y, c))


STEPS = {"y+": along_y(1), "y-": along_y(-1), "y2": along_y(2)}
for name, d in (("+", 1), ("-", -1), ("2", 2)):
    STEPS["f" + name] = crossed(d, 0)
    STEPS["g" + name] = crossed(d, 1)
STEPS["c"] = shift(lambda z, x, y, c: (z, x, y, c + 1))


def send(value, way):
    return lax.ppermute(value, ("req", "mlp"), STEPS[way])


def after(value, *first):
    return lax.optimization_barrier((value, first))[0]


def any_spec(n=1):
    return [pl.BlockSpec(memory_space=pl.ANY)] * n


def pinned(*arrays):
    return [pltpu.with_memory_space_constraint(a, pltpu.HBM) for a in arrays]


def hbm(n=1):
    return [pl.BlockSpec(memory_space=pltpu.HBM)] * n


SMEM = pl.BlockSpec(memory_space=pltpu.SMEM)


def first_body(where, up, down, docs, lengths, out, held, turned, limits, sems):
    index = where[4]
    lanes = pl.ds(pl.multiple_of(256 + (index >> 1) * LANES, LANES), LANES)
    copies = [pltpu.make_async_copy(w.at[:, lanes], held.at[k], sems.at[k]) for k, w in enumerate((up, down))]
    tokens = DOC_ROWS - 16
    copies.append(pltpu.make_async_copy(docs, out.at[PART : PART + tokens], sems.at[2]))
    copies.append(pltpu.make_async_copy(lengths, limits, sems.at[3]))
    for copy in copies:
        copy.start()
    start = pl.multiple_of((index & 1) * SLICE, SLICE)
    for k in range(2):
        copies[k].wait()
        for j in range(HALF):
            slab = k * HALF + j
            turned[slab] = held[k, j * LANES : (j + 1) * LANES, :].T
            out[slab * SLICE : (slab + 1) * SLICE, :] = turned[slab, pl.ds(start, SLICE), :]
    copies[3].wait()
    row = lax.broadcasted_iota(jnp.int32, (16, LANES), 0)
    limit = jnp.zeros((16, LANES), f32)
    for j in range(8):
        limit = jnp.where(row == j, limits[j].astype(f32), limit)
    out[PART + tokens : BLOCK, :] = limit.astype(bf16)
    copies[2].wait()


def first(where, up, down, docs, lengths):
    return pl.pallas_call(
        first_body,
        out_shape=jax.ShapeDtypeStruct((BLOCK, LANES), bf16),
        in_specs=[SMEM] + hbm(4),
        out_specs=vmem()[0],
        scratch_shapes=[
            pltpu.VMEM((2, D, LANES), bf16),
            pltpu.VMEM((SLABS, LANES, LANES), bf16),
            pltpu.SMEM((8,), jnp.int32),
            pltpu.SemaphoreType.DMA((4,)),
        ],
        compiler_params=params(16),
        cost_estimate=LIGHT,
        name="first",
    )(where, *pinned(up, down, docs, lengths))


def pack_body(up, down, low, high, held, sems):
    copies = [
        pltpu.make_async_copy(w.at[h * 512 : (h + 1) * 512], held.at[k, h * 512 : (h + 1) * 512], sems.at[2 * k + h])
        for k, w in enumerate((up, down))
        for h in range(2)
    ]
    for copy in copies:
        copy.start()
    for k in range(2):
        for j in range(HALF):
            if j % 4 == 0:
                copies[2 * k + j // 4].wait()
            rows = slice(j * LANES, (j + 1) * LANES)
            low[k * HALF + j] = held[k, rows, :256].T
            high[k * HALF + j] = held[k, rows, 256:].T


def pack(up, down):
    piece = jax.ShapeDtypeStruct((SLABS, 256, LANES), bf16)
    low, high = pl.pallas_call(
        pack_body,
        out_shape=(piece, piece),
        in_specs=hbm(2),
        out_specs=tuple(vmem(2)),
        scratch_shapes=[pltpu.VMEM((2, D, 512), bf16), pltpu.SemaphoreType.DMA((4,))],
        compiler_params=params(16),
        cost_estimate=LIGHT,
        name="pack",
    )(*pinned(up, down))
    return low.reshape(-1, LANES), high.reshape(-1, LANES)


def join_body(takes, *refs):
    out, at = refs[-1], 0
    for k, start, size in takes:
        out[at : at + size, :] = refs[k][start : start + size, :]
        at += size


def join(arrays, takes, name):
    return pl.pallas_call(
        functools.partial(join_body, takes),
        out_shape=jax.ShapeDtypeStruct((sum(t[2] for t in takes), LANES), bf16),
        in_specs=vmem(len(arrays)),
        out_specs=vmem()[0],
        compiler_params=params(16),
        cost_estimate=LIGHT,
        name=name,
    )(*arrays)


def attend_body(length, tok_hbm, qkv, wo_hbm, gain, out, packed, context, tok, held, wo, sems):
    rows_all = tok.shape[0]
    step = 512
    copies = [pltpu.make_async_copy(tok_hbm, tok, sems.at[6])]
    for i in range(6):
        columns = slice(i * step, (i + 1) * step)
        copies.append(pltpu.make_async_copy(qkv.at[:, columns], held.at[:, columns], sems.at[i]))
    copies.append(pltpu.make_async_copy(wo_hbm, wo, sems.at[7]))
    for copy in copies:
        copy.start()
    copies[0].wait()
    for i in range(6):
        columns = slice(i * step, (i + 1) * step)
        copies[1 + i].wait()
        packed[:, columns] = dot(tok[...], held[:, columns]).astype(bf16)
    lane = lax.broadcasted_iota(jnp.int32, (2 * SEQ, LANES), 1)
    low = lax.broadcasted_iota(jnp.int32, (SEQ, LANES), 1) < HD

    def request(r, carry):
        rows = pl.ds(pl.multiple_of(r * SEQ, SEQ), SEQ)
        live = lane < length[r]
        for p in range(HEADS // 2):
            at = p * LANES
            q = packed[rows, at : at + LANES]
            k = packed[rows, D + at : D + at + LANES]
            v = packed[rows, 2 * D + at : 2 * D + at + LANES]
            zero = jnp.zeros_like(q)
            both = jnp.concatenate([jnp.where(low, q, zero), jnp.where(low, zero, q)], axis=0)
            logits = jnp.where(live, dot_t(both, k) * HD ** (-0.5), DEAD)
            weights = jnp.exp(logits - jnp.max(logits, axis=-1, keepdims=True))
            probs = (weights * (1.0 / jnp.sum(weights, axis=-1, keepdims=True))).astype(bf16)
            ctx = dot(probs, v)
            context[rows, at : at + LANES] = jnp.where(low, ctx[:SEQ], ctx[SEQ:]).astype(bf16)
        return carry

    lax.fori_loop(0, rows_all // SEQ, request, 0)
    copies[7].wait()
    attended = dot(context[...], wo[...])
    out[...] = norm_rows(tok[...].astype(f32) + attended, gain[...]).astype(bf16)


def attend(tokens, qkv, wo, gain, length):
    rows = tokens.shape[0]
    return pl.pallas_call(
        attend_body,
        out_shape=jax.ShapeDtypeStruct((rows, D), bf16),
        in_specs=[SMEM] + hbm(3) + vmem(1),
        out_specs=vmem()[0],
        scratch_shapes=[
            pltpu.VMEM((rows, 3 * D), bf16),
            pltpu.VMEM((rows, D), bf16),
            pltpu.VMEM((rows, D), bf16),
            pltpu.VMEM((D, 3 * D), bf16),
            pltpu.VMEM((D, D), bf16),
            pltpu.SemaphoreType.DMA((8,)),
        ],
        compiler_params=params(32),
        cost_estimate=LIGHT,
        name="attend",
    )(length, *pinned(tokens, qkv, wo), gain.reshape(1, D))


def units(refs, half, start, size):
    slabs = []
    for j in range(HALF):
        parts, at = [], 0
        for ref, base, count in refs:
            low, high = max(start, at), min(start + size, at + count)
            if low < high:
                row = base + (half * HALF + j) * count
                parts.append(ref[row + low - at : row + high - at, :])
            at += count
        slabs.append(parts[0] if len(parts) == 1 else jnp.concatenate(parts, axis=0))
    return jnp.concatenate(slabs, axis=1)


def ffn_body(pieces, arrays, sets, fresh, *refs):
    inner, outs = refs[-1], refs[-1 - sets : -1]
    tokens, olds = refs[:sets], refs[sets : 2 * sets]
    held = refs[-1 - sets - arrays : -1 - sets]
    laid = [(held[k], base, count) for k, base, count in pieces]
    total = sum(count for _, _, count in pieces)
    for t in range(sets):
        x = tokens[t][...]
        for s in range(0, total, 256):
            n = min(256, total - s)
            inner[t, :, s : s + n] = gelu(dot_t(x, units(laid, 0, s, n))).astype(bf16)
    down = units(laid, 1, 0, total)
    for t in range(sets):
        for c in range(0, D, 256):
            more = dot(inner[t], down[:, c : c + 256])
            outs[t][:, c : c + 256] = more if fresh else olds[t][:, c : c + 256] + more


def ffn(tokens, olds, arrays, pieces, name):
    sets, rows = len(tokens), tokens[0].shape[0]
    total = sum(count for _, _, count in pieces)
    tail = tuple(tokens) + tuple(olds) + tuple(arrays)
    return pl.pallas_call(
        functools.partial(ffn_body, tuple(pieces), len(arrays), sets, not olds),
        out_shape=(jax.ShapeDtypeStruct((rows, D), f32),) * sets,
        in_specs=vmem(len(tail)),
        out_specs=tuple(vmem(sets)),
        input_output_aliases={sets + t: t for t in range(len(olds))},
        scratch_shapes=[pltpu.VMEM((sets, rows, total), bf16)],
        compiler_params=params(20),
        cost_estimate=LIGHT,
        name=name,
    )(*tail)


def embed_body(length, normed, mine, other, gain, we, out, kept):
    layer = norm_rows(normed[...].astype(f32) + (mine[...] + other[...]), gain[...]).astype(bf16)
    projected = dot(layer, we[...])
    unit = projected * lax.rsqrt(jnp.sum(projected * projected, axis=-1, keepdims=True) + 1e-06)
    slot = lax.broadcasted_iota(jnp.int32, (SEQ, P_SIZE), 0)
    for r in range(normed.shape[0] // SEQ):
        rows = slice(r * SEQ, (r + 1) * SEQ)
        live = jnp.where(slot < length[r], unit[rows], 0.0).astype(bf16)
        out[rows, :] = live
        kept[rows, :] = live


def embed(length, normed, mine, other, gain, we):
    shape = jax.ShapeDtypeStruct((normed.shape[0], P_SIZE), bf16)
    return pl.pallas_call(
        embed_body,
        out_shape=(shape, shape),
        in_specs=[SMEM] + vmem(5),
        out_specs=tuple(vmem(2)),
        compiler_params=params(24),
        cost_estimate=LIGHT,
        name="embed",
    )(length, normed, mine, other, gain.reshape(1, D), we)


def final_body(mine, other, out):
    out[...] = jnp.sum(jnp.maximum(mine[...], other[...]), axis=-1)


def final(mine, other, requests):
    picks = mine.shape[0] // requests
    shape = (requests, picks, mine.shape[1])
    return pl.pallas_call(
        final_body,
        out_shape=jax.ShapeDtypeStruct((requests, picks), f32),
        in_specs=vmem(2),
        out_specs=vmem()[0],
        compiler_params=params(8),
        cost_estimate=LIGHT,
        name="final",
    )(mine.reshape(shape), other.reshape(shape))


def score_body(where, cand, pair, emb, sib, *refs):
    docs, outs, held, sem = refs[:5], refs[5:7], refs[7], refs[8]
    copies = [pltpu.make_async_copy(docs[i], held.at[i], sem.at[i]) for i in range(3)]
    copies += [
        pltpu.make_async_copy(docs[3 + i], held.at[3, 2 * i : 2 * i + 2], sem.at[3 + i]) for i in range(2)
    ]
    for copy in copies:
        copy.start()
    z, x, y, c = where[0], where[1], where[2], where[3]
    local = lax.broadcasted_iota(jnp.int32, (TOKS, LANES), 0)
    pos = jnp.concatenate(
        [local + TOKS * (2 * ((y + d) & 3) + c) for d in AROUND_Y], axis=0
    ).astype(f32)
    row = lax.broadcasted_iota(jnp.int32, (16, LANES), 0)

    def slot(d):
        return jnp.where(d == 0, 0, jnp.where(d == 3, 1, d + 1))

    for copy in copies:
        copy.wait()
    per = cand.shape[0]
    for i in range(2 * per):
        e = cand[i] if i < per else pair[i - per]
        tokens = emb if i < per else sib
        j, req = e & 7, e >> 3
        sz, sx = slot(((req >> 2) - z) & 3), slot(((req & 3) - x) & 3)
        outer = jnp.where(c == 0, sz, sx)
        within = jnp.where(c == 0, sx, sz)
        block = held[outer, within, :, pl.ds(pl.multiple_of(j * TOKS, TOKS), TOKS), :]
        lens = held[outer, within, 0, 8 * TOKS : DOC_ROWS, :].astype(f32)
        limit = jnp.sum(jnp.where(row == j, lens, 0.0), axis=0, keepdims=True)
        r = (i % per) // 8
        sims = dot_t(block.reshape(4 * TOKS, P_SIZE), tokens[r * SEQ : (r + 1) * SEQ, :])
        at = i % per
        outs[i // per][at : at + 1, :] = jnp.max(jnp.where(pos < limit, sims, DEAD), axis=0, keepdims=True)


def score(where, cand, pair, emb, sib, docs):
    total = cand.size
    docs = [d.reshape(-1, 4, DOC_ROWS, P_SIZE) for d in docs]
    return pl.pallas_call(
        score_body,
        out_shape=(jax.ShapeDtypeStruct((total, SEQ), f32),) * 2,
        in_specs=[SMEM] * 3 + vmem(2) + any_spec(5),
        out_specs=tuple(vmem(2)),
        scratch_shapes=[
            pltpu.VMEM((4, 4, 4, DOC_ROWS, P_SIZE), bf16),
            pltpu.SemaphoreType.DMA((5,)),
        ],
        compiler_params=params(16),
        cost_estimate=LIGHT,
        name="score",
    )(where, cand.reshape(-1), pair.reshape(-1), emb, sib, *docs)


def on_device(
    tokens,
    attend_weight,
    output_weight,
    attend_gain,
    up_weight,
    down_weight,
    mlp_gain,
    embed_weight,
    query_length,
    documents,
    document_length,
    candidates,
):
    req, mlp = lax.axis_index("req"), lax.axis_index("mlp")
    z, x, y, c = req // 4, req % 4, mlp // 2, mlp % 2
    where = jnp.stack([z, x, y, c, jnp.where(c == 0, x, z)]).astype(jnp.int32)
    start = first(where, up_weight, down_weight, documents.reshape(-1, P_SIZE), document_length)
    near = [send(start, way) for way in ("y+", "y-", "y2")]
    low, high = pack(up_weight, down_weight)
    normed = attend(tokens, attend_weight, output_weight, after(attend_gain, start), query_length)
    near = after(tuple(near), normed, high)

    whole = [(k, 0, BLOCK) for k in range(3)] + [(3, PART, DOC_ROWS)]
    go = join([*near, start], whole, "join1")
    came = [send(go, way) for way in ("f+", "f-", "f2")]
    pair_normed = send(after(normed, go), "c")
    pair = send(after(candidates, go), "c")
    low_go = after(low, pair_normed, pair)
    low_near = [send(low_go, "y+"), send(low_go, "y-")]
    sets = (normed, pair_normed)
    total = ffn(sets, (), [low, high], [(0, 0, 256), (1, 0, 256)], "ffn1")
    parts = [(i * BLOCK, SLICE) for i in range(3)]
    pieces = [(k, 0, SLICE) for k in range(3)] + [(3,) + p for p in parts]
    total = ffn(sets, total, [*near, came[0]], pieces, "ffn2")
    came, low_near, total = after((came, low_near, total), *total)
    takes = [(k, at, DOC_ROWS) for k in range(4) for at in [i * BLOCK + PART for i in range(3)] + [3 * BLOCK]]
    docs = join([go, *came], takes, "join2")
    last = [send(docs, way) for way in ("g+", "g-")]
    mid = 128
    ahead = join([low_near[0]], [(0, k * 256, mid) for k in range(SLABS)], "join5")
    behind = join([low_near[1]], [(0, k * 256 + mid, mid) for k in range(SLABS)], "join6")
    low_far = [send(ahead, "y+"), send(behind, "y-")]
    pieces = [(k,) + p for k in range(2) for p in parts] + [(2, 0, 256), (3, 0, 256)]
    total = ffn(sets, total, [*came[1:], *low_near], pieces, "ffn3")
    cut = docs.shape[0] // 2
    last += [
        send(join([last[0]], [(0, 0, cut)], "join3"), "g+"),
        send(join([last[1]], [(0, cut, cut)], "join4"), "g-"),
    ]
    low_far = after(low_far, *last[:2])
    rest = [(0, 0, mid), (1, 0, mid)]
    away, = ffn(sets[1:], total[1:], low_far, rest, "ffn4")
    other = send(away, "c")
    mine, = ffn(sets[:1], total[:1], low_far, rest, "ffn5")
    embedded, kept = embed(query_length, normed, mine, other, mlp_gain, embed_weight)
    sib = send(kept, "c")
    best, best_pair = score(where, candidates, pair, kept, sib, [docs] + last)
    scores = final(best, send(best_pair, "c"), candidates.shape[0])
    return (embedded, scores)


def solution(mesh):
    return jax.shard_map(
        on_device,
        mesh=mesh,
        in_specs=(
            P(("req", "mlp"), None),
            P(),
            P(),
            P(),
            P(None, "mlp"),
            P(None, "mlp"),
            P(),
            P(),
            P(("req", "mlp")),
            P("req", "mlp", None),
            P("req"),
            P(("req", "mlp"), None),
        ),
        out_specs=(P(("req", "mlp"), None), P(("req", "mlp"), None)),
        check_vma=False,
    )
```

```python
import functools

import jax
import jax.numpy as jnp
from jax import lax
from jax.experimental import pallas as pl
from jax.experimental.pallas import tpu as pltpu
from jax.sharding import PartitionSpec as P

D = 1024
HEADS = 16
HD = 64
P_SIZE = 128
SEQ = 128
LANES = 128
SLABS = 2 * D // LANES
HALF = SLABS // 2
TOKS = 32
DOC_ROWS = 272
SLICE = 64
PART = SLABS * SLICE
BLOCK = PART + DOC_ROWS
AROUND = (0, 3, 1, 2)
AROUND_Y = (3, 1, 2, 0)
DEAD = -1e30
f32 = jnp.float32
bf16 = jnp.bfloat16


def dot(a, b):
    return jnp.dot(a, b, preferred_element_type=f32)


def dot_t(a, b):
    return lax.dot_general(a, b, (((1,), (1,)), ((), ())), preferred_element_type=f32)


def norm_rows(values, scaling):
    average = jnp.mean(values, axis=-1, keepdims=True)
    centred = values - average
    variance = jnp.mean(centred * centred, axis=-1, keepdims=True)
    return centred * lax.rsqrt(variance + 1e-05) * scaling


def gelu(x):
    return 0.5 * x * (1.0 + lax.erf(x * (0.5 ** 0.5)))


LIGHT = pl.CostEstimate(flops=1, transcendentals=0, bytes_accessed=1)


def params(mib):
    return pltpu.CompilerParams(vmem_limit_bytes=mib * 1024 * 1024)


def vmem(n=1):
    return [pl.BlockSpec(memory_space=pltpu.VMEM)] * n


def place(z, x, y, c):
    return ((z % 4) * 4 + x % 4) * 8 + (y % 4) * 2 + c % 2


def shift(move):
    return [
        (place(z, x, y, c), place(*move(z, x, y, c)))
        for z in range(4)
        for x in range(4)
        for y in range(4)
        for c in range(2)
    ]


def along_y(d):
    return shift(lambda z, x, y, c: (z, x, y + d, c))


def crossed(d, first):
    return shift(lambda z, x, y, c: (z, x + d, y, c) if c == first else (z + d, x, y, c))


STEPS = {"y+": along_y(1), "y-": along_y(-1), "y2": along_y(2)}
for name, d in (("+", 1), ("-", -1), ("2", 2)):
    STEPS["f" + name] = crossed(d, 0)
    STEPS["g" + name] = crossed(d, 1)
STEPS["c"] = shift(lambda z, x, y, c: (z, x, y, c + 1))


def send(value, way):
    return lax.ppermute(value, ("req", "mlp"), STEPS[way])


def after(value, *first):
    return lax.optimization_barrier((value, first))[0]


def any_spec(n=1):
    return [pl.BlockSpec(memory_space=pl.ANY)] * n


def pinned(*arrays):
    return [pltpu.with_memory_space_constraint(a, pltpu.HBM) for a in arrays]


def hbm(n=1):
    return [pl.BlockSpec(memory_space=pltpu.HBM)] * n


SMEM = pl.BlockSpec(memory_space=pltpu.SMEM)


def first_body(where, up, down, docs, lengths, out, held, turned, limits, sems):
    index = where[4]
    lanes = pl.ds(pl.multiple_of(256 + (index >> 1) * LANES, LANES), LANES)
    copies = [pltpu.make_async_copy(w.at[:, lanes], held.at[k], sems.at[k]) for k, w in enumerate((up, down))]
    tokens = DOC_ROWS - 16
    copies.append(pltpu.make_async_copy(docs, out.at[PART : PART + tokens], sems.at[2]))
    copies.append(pltpu.make_async_copy(lengths, limits, sems.at[3]))
    for copy in copies:
        copy.start()
    start = pl.multiple_of((index & 1) * SLICE, SLICE)
    for k in range(2):
        copies[k].wait()
        for j in range(HALF):
            slab = k * HALF + j
            turned[slab] = held[k, j * LANES : (j + 1) * LANES, :].T
            out[slab * SLICE : (slab + 1) * SLICE, :] = turned[slab, pl.ds(start, SLICE), :]
    copies[3].wait()
    row = lax.broadcasted_iota(jnp.int32, (16, LANES), 0)
    limit = jnp.zeros((16, LANES), f32)
    for j in range(8):
        limit = jnp.where(row == j, limits[j].astype(f32), limit)
    out[PART + tokens : BLOCK, :] = limit.astype(bf16)
    copies[2].wait()


def first(where, up, down, docs, lengths):
    return pl.pallas_call(
        first_body,
        out_shape=jax.ShapeDtypeStruct((BLOCK, LANES), bf16),
        in_specs=[SMEM] + hbm(4),
        out_specs=vmem()[0],
        scratch_shapes=[
            pltpu.VMEM((2, D, LANES), bf16),
            pltpu.VMEM((SLABS, LANES, LANES), bf16),
            pltpu.SMEM((8,), jnp.int32),
            pltpu.SemaphoreType.DMA((4,)),
        ],
        compiler_params=params(8),
        cost_estimate=LIGHT,
        name="first",
    )(where, *pinned(up, down, docs, lengths))


def pack_body(up, down, low, high, held, sems):
    copies = [
        pltpu.make_async_copy(w.at[h * 512 : (h + 1) * 512], held.at[k, h * 512 : (h + 1) * 512], sems.at[2 * k + h])
        for k, w in enumerate((up, down))
        for h in range(2)
    ]
    for copy in copies:
        copy.start()
    for k in range(2):
        for j in range(HALF):
            if j % 4 == 0:
                copies[2 * k + j // 4].wait()
            rows = slice(j * LANES, (j + 1) * LANES)
            low[k * HALF + j] = held[k, rows, :256].T
            high[k * HALF + j] = held[k, rows, 256:].T


def pack(up, down):
    piece = jax.ShapeDtypeStruct((SLABS, 256, LANES), bf16)
    low, high = pl.pallas_call(
        pack_body,
        out_shape=(piece, piece),
        in_specs=hbm(2),
        out_specs=tuple(vmem(2)),
        scratch_shapes=[pltpu.VMEM((2, D, 512), bf16), pltpu.SemaphoreType.DMA((4,))],
        compiler_params=params(8),
        cost_estimate=LIGHT,
        name="pack",
    )(*pinned(up, down))
    return low.reshape(-1, LANES), high.reshape(-1, LANES)


def join_body(takes, *refs):
    out, at = refs[-1], 0
    for k, start, size in takes:
        out[at : at + size, :] = refs[k][start : start + size, :]
        at += size


def join(arrays, takes, name):
    return pl.pallas_call(
        functools.partial(join_body, takes),
        out_shape=jax.ShapeDtypeStruct((sum(t[2] for t in takes), LANES), bf16),
        in_specs=vmem(len(arrays)),
        out_specs=vmem()[0],
        compiler_params=params(16),
        cost_estimate=LIGHT,
        name=name,
    )(*arrays)


def attend_body(length, tok_hbm, qkv, wo_hbm, gain, out, packed, context, tok, held, wo, sems):
    rows_all = tok.shape[0]
    step = 512
    copies = [pltpu.make_async_copy(tok_hbm, tok, sems.at[6])]
    for i in range(6):
        columns = slice(i * step, (i + 1) * step)
        copies.append(pltpu.make_async_copy(qkv.at[:, columns], held.at[:, columns], sems.at[i]))
    copies.append(pltpu.make_async_copy(wo_hbm, wo, sems.at[7]))
    for copy in copies[:3]:
        copy.start()
    copies[0].wait()
    for i in range(6):
        columns = slice(i * step, (i + 1) * step)
        copies[1 + i].wait()
        if i < 5:
            copies[3 + i].start()
        packed[:, columns] = dot(tok[...], held[:, columns]).astype(bf16)
    lane = lax.broadcasted_iota(jnp.int32, (2 * SEQ, LANES), 1)
    low = lax.broadcasted_iota(jnp.int32, (SEQ, LANES), 1) < HD

    def request(r, carry):
        rows = pl.ds(pl.multiple_of(r * SEQ, SEQ), SEQ)
        live = lane < length[r]
        for p in range(HEADS // 2):
            at = p * LANES
            q = packed[rows, at : at + LANES]
            k = packed[rows, D + at : D + at + LANES]
            v = packed[rows, 2 * D + at : 2 * D + at + LANES]
            zero = jnp.zeros_like(q)
            both = jnp.concatenate([jnp.where(low, q, zero), jnp.where(low, zero, q)], axis=0)
            logits = jnp.where(live, dot_t(both, k) * HD ** (-0.5), DEAD)
            weights = jnp.exp(logits - jnp.max(logits, axis=-1, keepdims=True))
            probs = (weights * (1.0 / jnp.sum(weights, axis=-1, keepdims=True))).astype(bf16)
            ctx = dot(probs, v)
            context[rows, at : at + LANES] = jnp.where(low, ctx[:SEQ], ctx[SEQ:]).astype(bf16)
        return carry

    lax.fori_loop(0, rows_all // SEQ, request, 0)
    copies[7].wait()
    attended = dot(context[...], wo[...])
    out[...] = norm_rows(tok[...].astype(f32) + attended, gain[...]).astype(bf16)


def attend(tokens, qkv, wo, gain, length):
    rows = tokens.shape[0]
    return pl.pallas_call(
        attend_body,
        out_shape=jax.ShapeDtypeStruct((rows, D), bf16),
        in_specs=[SMEM] + hbm(3) + vmem(1),
        out_specs=vmem()[0],
        scratch_shapes=[
            pltpu.VMEM((rows, 3 * D), bf16),
            pltpu.VMEM((rows, D), bf16),
            pltpu.VMEM((rows, D), bf16),
            pltpu.VMEM((D, 3 * D), bf16),
            pltpu.VMEM((D, D), bf16),
            pltpu.SemaphoreType.DMA((8,)),
        ],
        compiler_params=params(24),
        cost_estimate=LIGHT,
        name="attend",
    )(length, *pinned(tokens, qkv, wo), gain.reshape(1, D))


def units(refs, half, start, size):
    slabs = []
    for j in range(HALF):
        parts, at = [], 0
        for ref, base, count in refs:
            low, high = max(start, at), min(start + size, at + count)
            if low < high:
                row = base + (half * HALF + j) * count
                parts.append(ref[row + low - at : row + high - at, :])
            at += count
        slabs.append(parts[0] if len(parts) == 1 else jnp.concatenate(parts, axis=0))
    return jnp.concatenate(slabs, axis=1)


def ffn_body(pieces, arrays, sets, fresh, *refs):
    inner, outs = refs[-1], refs[-1 - sets : -1]
    tokens, olds = refs[:sets], refs[sets : 2 * sets]
    held = refs[-1 - sets - arrays : -1 - sets]
    laid = [(held[k], base, count) for k, base, count in pieces]
    total = sum(count for _, _, count in pieces)
    for t in range(sets):
        x = tokens[t][...]
        for s in range(0, total, 256):
            n = min(256, total - s)
            inner[t, :, s : s + n] = gelu(dot_t(x, units(laid, 0, s, n))).astype(bf16)
    down = units(laid, 1, 0, total)
    for t in range(sets):
        for c in range(0, D, 256):
            more = dot(inner[t], down[:, c : c + 256])
            outs[t][:, c : c + 256] = more if fresh else olds[t][:, c : c + 256] + more


def ffn(tokens, olds, arrays, pieces, name):
    sets, rows = len(tokens), tokens[0].shape[0]
    total = sum(count for _, _, count in pieces)
    tail = tuple(tokens) + tuple(olds) + tuple(arrays)
    return pl.pallas_call(
        functools.partial(ffn_body, tuple(pieces), len(arrays), sets, not olds),
        out_shape=(jax.ShapeDtypeStruct((rows, D), f32),) * sets,
        in_specs=vmem(len(tail)),
        out_specs=tuple(vmem(sets)),
        input_output_aliases={sets + t: t for t in range(len(olds))},
        scratch_shapes=[pltpu.VMEM((sets, rows, total), bf16)],
        compiler_params=params(16),
        cost_estimate=LIGHT,
        name=name,
    )(*tail)


def embed_body(length, normed, mine, other, gain, we, out, kept):
    layer = norm_rows(normed[...].astype(f32) + (mine[...] + other[...]), gain[...]).astype(bf16)
    projected = dot(layer, we[...])
    unit = projected * lax.rsqrt(jnp.sum(projected * projected, axis=-1, keepdims=True) + 1e-06)
    slot = lax.broadcasted_iota(jnp.int32, (SEQ, P_SIZE), 0)
    for r in range(normed.shape[0] // SEQ):
        rows = slice(r * SEQ, (r + 1) * SEQ)
        live = jnp.where(slot < length[r], unit[rows], 0.0).astype(bf16)
        out[rows, :] = live
        kept[rows, :] = live


def embed(length, normed, mine, other, gain, we):
    shape = jax.ShapeDtypeStruct((normed.shape[0], P_SIZE), bf16)
    return pl.pallas_call(
        embed_body,
        out_shape=(shape, shape),
        in_specs=[SMEM] + vmem(5),
        out_specs=tuple(vmem(2)),
        compiler_params=params(12),
        cost_estimate=LIGHT,
        name="embed",
    )(length, normed, mine, other, gain.reshape(1, D), we)


def final_body(mine, other, out):
    out[...] = jnp.sum(jnp.maximum(mine[...], other[...]), axis=-1)


def final(mine, other, requests):
    picks = mine.shape[0] // requests
    shape = (requests, picks, mine.shape[1])
    return pl.pallas_call(
        final_body,
        out_shape=jax.ShapeDtypeStruct((requests, picks), f32),
        in_specs=vmem(2),
        out_specs=vmem()[0],
        compiler_params=params(8),
        cost_estimate=LIGHT,
        name="final",
    )(mine.reshape(shape), other.reshape(shape))


def score_body(where, cand, pair, emb, sib, *refs):
    docs, outs, held, sem = refs[:5], refs[5:7], refs[7], refs[8]
    copies = [pltpu.make_async_copy(docs[i], held.at[i], sem.at[i]) for i in range(3)]
    copies += [
        pltpu.make_async_copy(docs[3 + i], held.at[3, 2 * i : 2 * i + 2], sem.at[3 + i]) for i in range(2)
    ]
    for copy in copies:
        copy.start()
    z, x, y, c = where[0], where[1], where[2], where[3]
    local = lax.broadcasted_iota(jnp.int32, (TOKS, LANES), 0)
    pos = jnp.concatenate(
        [local + TOKS * (2 * ((y + d) & 3) + c) for d in AROUND_Y], axis=0
    ).astype(f32)
    row = lax.broadcasted_iota(jnp.int32, (16, LANES), 0)

    def slot(d):
        return jnp.where(d == 0, 0, jnp.where(d == 3, 1, d + 1))

    for copy in copies:
        copy.wait()
    per = cand.shape[0]
    for i in range(2 * per):
        e = cand[i] if i < per else pair[i - per]
        tokens = emb if i < per else sib
        j, req = e & 7, e >> 3
        sz, sx = slot(((req >> 2) - z) & 3), slot(((req & 3) - x) & 3)
        outer = jnp.where(c == 0, sz, sx)
        within = jnp.where(c == 0, sx, sz)
        block = held[outer, within, :, pl.ds(pl.multiple_of(j * TOKS, TOKS), TOKS), :]
        lens = held[outer, within, 0, 8 * TOKS : DOC_ROWS, :].astype(f32)
        limit = jnp.sum(jnp.where(row == j, lens, 0.0), axis=0, keepdims=True)
        r = (i % per) // 8
        sims = dot_t(block.reshape(4 * TOKS, P_SIZE), tokens[r * SEQ : (r + 1) * SEQ, :])
        at = i % per
        outs[i // per][at : at + 1, :] = jnp.max(jnp.where(pos < limit, sims, DEAD), axis=0, keepdims=True)


def score(where, cand, pair, emb, sib, docs):
    total = cand.size
    docs = [d.reshape(-1, 4, DOC_ROWS, P_SIZE) for d in docs]
    return pl.pallas_call(
        score_body,
        out_shape=(jax.ShapeDtypeStruct((total, SEQ), f32),) * 2,
        in_specs=[SMEM] * 3 + vmem(2) + any_spec(5),
        out_specs=tuple(vmem(2)),
        scratch_shapes=[
            pltpu.VMEM((4, 4, 4, DOC_ROWS, P_SIZE), bf16),
            pltpu.SemaphoreType.DMA((5,)),
        ],
        compiler_params=params(8),
        cost_estimate=LIGHT,
        name="score",
    )(where, cand.reshape(-1), pair.reshape(-1), emb, sib, *docs)


def on_device(
    tokens,
    attend_weight,
    output_weight,
    attend_gain,
    up_weight,
    down_weight,
    mlp_gain,
    embed_weight,
    query_length,
    documents,
    document_length,
    candidates,
):
    req, mlp = lax.axis_index("req"), lax.axis_index("mlp")
    z, x, y, c = req // 4, req % 4, mlp // 2, mlp % 2
    where = jnp.stack([z, x, y, c, jnp.where(c == 0, x, z)]).astype(jnp.int32)
    start = first(where, up_weight, down_weight, documents.reshape(-1, P_SIZE), document_length)
    near = [send(start, way) for way in ("y+", "y-", "y2")]
    low, high = pack(up_weight, down_weight)
    normed = attend(tokens, attend_weight, output_weight, after(attend_gain, start), query_length)
    pair = send(after(candidates, start), "c")
    near, pair = after((tuple(near), pair), normed, high)

    whole = [(k, 0, BLOCK) for k in range(3)] + [(3, PART, DOC_ROWS)]
    go = join([*near, start], whole, "join1")
    came = [send(go, way) for way in ("f+", "f-", "f2")]
    pair_normed = send(after(normed, go), "c")
    low_go = after(low, pair_normed)
    low_near = [send(low_go, "y+"), send(low_go, "y-")]
    sets = (normed, pair_normed)
    total = ffn(sets, (), [low, high], [(0, 0, 256), (1, 0, 256)], "ffn1")
    parts = [(i * BLOCK, SLICE) for i in range(3)]
    pieces = [(k, 0, SLICE) for k in range(3)] + [(3,) + p for p in parts]
    total = ffn(sets, total, [*near, came[0]], pieces, "ffn2")
    came, total = after((came, total), *total)
    takes = [(k, at, DOC_ROWS) for k in range(4) for at in [i * BLOCK + PART for i in range(3)] + [3 * BLOCK]]
    docs = join([go, *came], takes, "join2")
    last = [send(docs, way) for way in ("g+", "g-")]
    mid = 128
    low_near = after(tuple(low_near), docs)
    ahead = join([low_near[0]], [(0, k * 256, mid) for k in range(SLABS)], "join5")
    behind = join([low_near[1]], [(0, k * 256 + mid, mid) for k in range(SLABS)], "join6")
    low_far = [send(ahead, "y+"), send(behind, "y-")]
    pieces = [(k,) + p for k in range(2) for p in parts] + [(2, 0, 256), (3, 0, 256)]
    total = ffn(sets, total, [*came[1:], *low_near], pieces, "ffn3")
    cut = docs.shape[0] // 2
    halves = [join([last[0]], [(0, 0, cut)], "join3"), join([last[1]], [(0, cut, cut)], "join4")]
    last += [send(halves[0], "g+"), send(halves[1], "g-")]
    low_far = after(tuple(low_far), *halves)
    rest = [(0, 0, mid), (1, 0, mid)]
    away, = ffn(sets[1:], total[1:], low_far, rest, "ffn4")
    other = send(away, "c")
    mine, = ffn(sets[:1], total[:1], low_far, rest, "ffn5")
    embedded, kept = embed(query_length, normed, mine, other, mlp_gain, embed_weight)
    sib = send(kept, "c")
    best, best_pair = score(where, candidates, pair, kept, sib, [docs] + last)
    scores = final(best, send(best_pair, "c"), candidates.shape[0])
    return (embedded, scores)


def solution(mesh):
    return jax.shard_map(
        on_device,
        mesh=mesh,
        in_specs=(
            P(("req", "mlp"), None),
            P(),
            P(),
            P(),
            P(None, "mlp"),
            P(None, "mlp"),
            P(),
            P(),
            P(("req", "mlp")),
            P("req", "mlp", None),
            P("req"),
            P(("req", "mlp"), None),
        ),
        out_specs=(P(("req", "mlp"), None), P(("req", "mlp"), None)),
        check_vma=False,
    )
```

```python
import functools

import jax
import jax.numpy as jnp
from jax import lax
from jax.experimental import pallas as pl
from jax.experimental.pallas import tpu as pltpu
from jax.sharding import PartitionSpec as P

D = 1024
HEADS = 16
HD = 64
P_SIZE = 128
SEQ = 128
LANES = 128
SLABS = 2 * D // LANES
HALF = SLABS // 2
TOKS = 32
DOC_ROWS = 272
SLICE = 64
PART = SLABS * SLICE
BLOCK = PART + DOC_ROWS
AROUND = (0, 3, 1, 2)
AROUND_Y = (3, 1, 2, 0)
DEAD = -1e30
f32 = jnp.float32
bf16 = jnp.bfloat16


def dot(a, b):
    return jnp.dot(a, b, preferred_element_type=f32)


def dot_t(a, b):
    return lax.dot_general(a, b, (((1,), (1,)), ((), ())), preferred_element_type=f32)


def norm_rows(values, scaling):
    average = jnp.mean(values, axis=-1, keepdims=True)
    centred = values - average
    variance = jnp.mean(centred * centred, axis=-1, keepdims=True)
    return centred * lax.rsqrt(variance + 1e-05) * scaling


def gelu(x):
    return 0.5 * x * (1.0 + lax.erf(x * (0.5 ** 0.5)))


LIGHT = pl.CostEstimate(flops=1, transcendentals=0, bytes_accessed=1)


def params(mib):
    return pltpu.CompilerParams(vmem_limit_bytes=mib * 1024 * 1024)


def vmem(n=1):
    return [pl.BlockSpec(memory_space=pltpu.VMEM)] * n


def place(z, x, y, c):
    return ((z % 4) * 4 + x % 4) * 8 + (y % 4) * 2 + c % 2


def shift(move):
    return [
        (place(z, x, y, c), place(*move(z, x, y, c)))
        for z in range(4)
        for x in range(4)
        for y in range(4)
        for c in range(2)
    ]


def along_y(d):
    return shift(lambda z, x, y, c: (z, x, y + d, c))


def crossed(d, first):
    return shift(lambda z, x, y, c: (z, x + d, y, c) if c == first else (z + d, x, y, c))


STEPS = {"y+": along_y(1), "y-": along_y(-1), "y2": along_y(2)}
for name, d in (("+", 1), ("-", -1), ("2", 2)):
    STEPS["f" + name] = crossed(d, 0)
    STEPS["g" + name] = crossed(d, 1)
STEPS["c"] = shift(lambda z, x, y, c: (z, x, y, c + 1))


def send(value, way):
    return lax.ppermute(value, ("req", "mlp"), STEPS[way])


def after(value, *first):
    return lax.optimization_barrier((value, first))[0]


def any_spec(n=1):
    return [pl.BlockSpec(memory_space=pl.ANY)] * n


def pinned(*arrays):
    return [pltpu.with_memory_space_constraint(a, pltpu.HBM) for a in arrays]


def hbm(n=1):
    return [pl.BlockSpec(memory_space=pltpu.HBM)] * n


SMEM = pl.BlockSpec(memory_space=pltpu.SMEM)


def first_body(where, up, down, docs, lengths, out, held, turned, limits, sems):
    index = where[4]
    lanes = pl.ds(pl.multiple_of(256 + (index >> 1) * LANES, LANES), LANES)
    copies = [pltpu.make_async_copy(w.at[:, lanes], held.at[k], sems.at[k]) for k, w in enumerate((up, down))]
    tokens = DOC_ROWS - 16
    copies.append(pltpu.make_async_copy(docs, out.at[PART : PART + tokens], sems.at[2]))
    copies.append(pltpu.make_async_copy(lengths, limits, sems.at[3]))
    for copy in copies:
        copy.start()
    start = pl.multiple_of((index & 1) * SLICE, SLICE)
    for k in range(2):
        copies[k].wait()
        for j in range(HALF):
            slab = k * HALF + j
            turned[slab] = held[k, j * LANES : (j + 1) * LANES, :].T
            out[slab * SLICE : (slab + 1) * SLICE, :] = turned[slab, pl.ds(start, SLICE), :]
    copies[3].wait()
    row = lax.broadcasted_iota(jnp.int32, (16, LANES), 0)
    limit = jnp.zeros((16, LANES), f32)
    for j in range(8):
        limit = jnp.where(row == j, limits[j].astype(f32), limit)
    out[PART + tokens : BLOCK, :] = limit.astype(bf16)
    copies[2].wait()


def first(where, up, down, docs, lengths):
    return pl.pallas_call(
        first_body,
        out_shape=jax.ShapeDtypeStruct((BLOCK, LANES), bf16),
        in_specs=[SMEM] + hbm(4),
        out_specs=vmem()[0],
        scratch_shapes=[
            pltpu.VMEM((2, D, LANES), bf16),
            pltpu.VMEM((SLABS, LANES, LANES), bf16),
            pltpu.SMEM((8,), jnp.int32),
            pltpu.SemaphoreType.DMA((4,)),
        ],
        compiler_params=params(8),
        cost_estimate=LIGHT,
        name="first",
    )(where, *pinned(up, down, docs, lengths))


def join_body(takes, *refs):
    out, at = refs[-1], 0
    for k, start, size in takes:
        out[at : at + size, :] = refs[k][start : start + size, :]
        at += size


def join(arrays, takes, name):
    return pl.pallas_call(
        functools.partial(join_body, takes),
        out_shape=jax.ShapeDtypeStruct((sum(t[2] for t in takes), LANES), bf16),
        in_specs=vmem(len(arrays)),
        out_specs=vmem()[0],
        compiler_params=params(16),
        cost_estimate=LIGHT,
        name=name,
    )(*arrays)


def attend_body(
    length, tok_hbm, qkv, wo_hbm, up, down, gain, out, low_out, high_out, packed, context, tok, held, wo, wide, sems
):
    rows_all = tok.shape[0]
    step = 512
    copies = [pltpu.make_async_copy(tok_hbm, tok, sems.at[0])]
    for i in range(6):
        columns = slice(i * step, (i + 1) * step)
        copies.append(pltpu.make_async_copy(qkv.at[:, columns], held.at[:, columns], sems.at[1 + i]))
    copies.append(pltpu.make_async_copy(up, wide.at[0], sems.at[7]))
    copies.append(pltpu.make_async_copy(down, wide.at[1], sems.at[8]))
    copies.append(pltpu.make_async_copy(wo_hbm, wo, sems.at[9]))
    for copy in copies[:3]:
        copy.start()
    copies[0].wait()
    for i in range(6):
        columns = slice(i * step, (i + 1) * step)
        copies[1 + i].wait()
        copies[3 + i].start()
        packed[:, columns] = dot(tok[...], held[:, columns]).astype(bf16)
    copies[9].start()
    for k in range(2):
        copies[7 + k].wait()
        for j in range(HALF):
            rows = slice(j * LANES, (j + 1) * LANES)
            low_out[k * HALF + j] = wide[k, rows, :256].T
            high_out[k * HALF + j] = wide[k, rows, 256:].T
    lane = lax.broadcasted_iota(jnp.int32, (2 * SEQ, LANES), 1)
    low = lax.broadcasted_iota(jnp.int32, (SEQ, LANES), 1) < HD

    def request(r, carry):
        rows = pl.ds(pl.multiple_of(r * SEQ, SEQ), SEQ)
        live = lane < length[r]
        for p in range(HEADS // 2):
            at = p * LANES
            q = packed[rows, at : at + LANES]
            k = packed[rows, D + at : D + at + LANES]
            v = packed[rows, 2 * D + at : 2 * D + at + LANES]
            zero = jnp.zeros_like(q)
            both = jnp.concatenate([jnp.where(low, q, zero), jnp.where(low, zero, q)], axis=0)
            logits = jnp.where(live, dot_t(both, k) * HD ** (-0.5), DEAD)
            weights = jnp.exp(logits - jnp.max(logits, axis=-1, keepdims=True))
            probs = (weights * (1.0 / jnp.sum(weights, axis=-1, keepdims=True))).astype(bf16)
            ctx = dot(probs, v)
            context[rows, at : at + LANES] = jnp.where(low, ctx[:SEQ], ctx[SEQ:]).astype(bf16)
        return carry

    lax.fori_loop(0, rows_all // SEQ, request, 0)
    copies[9].wait()
    attended = dot(context[...], wo[...])
    out[...] = norm_rows(tok[...].astype(f32) + attended, gain[...]).astype(bf16)


def attend(tokens, qkv, wo, gain, length, up, down):
    rows = tokens.shape[0]
    piece = jax.ShapeDtypeStruct((SLABS, 256, LANES), bf16)
    normed, low, high = pl.pallas_call(
        attend_body,
        out_shape=(jax.ShapeDtypeStruct((rows, D), bf16), piece, piece),
        in_specs=[SMEM] + hbm(5) + vmem(1),
        out_specs=tuple(vmem(3)),
        scratch_shapes=[
            pltpu.VMEM((rows, 3 * D), bf16),
            pltpu.VMEM((rows, D), bf16),
            pltpu.VMEM((rows, D), bf16),
            pltpu.VMEM((D, 3 * D), bf16),
            pltpu.VMEM((D, D), bf16),
            pltpu.VMEM((2, D, 512), bf16),
            pltpu.SemaphoreType.DMA((10,)),
        ],
        compiler_params=params(28),
        cost_estimate=LIGHT,
        name="attend",
    )(length, *pinned(tokens, qkv, wo, up, down), gain.reshape(1, D))
    return normed, low.reshape(-1, LANES), high.reshape(-1, LANES)


def halves_body(plus, minus, low, high, sems):
    rows = low.shape[0]
    copies = [
        pltpu.make_async_copy(plus.at[:rows], low, sems.at[0]),
        pltpu.make_async_copy(minus.at[rows:], high, sems.at[1]),
    ]
    for copy in copies:
        copy.start()
    for copy in copies:
        copy.wait()


def halves(plus, minus):
    half = jax.ShapeDtypeStruct((plus.shape[0] // 2, LANES), bf16)
    return pl.pallas_call(
        halves_body,
        out_shape=(half, half),
        in_specs=any_spec(2),
        out_specs=tuple(any_spec(2)),
        scratch_shapes=[pltpu.SemaphoreType.DMA((2,))],
        compiler_params=params(8),
        cost_estimate=LIGHT,
        name="halves",
    )(plus, minus)


def units(refs, half, start, size):
    slabs = []
    for j in range(HALF):
        parts, at = [], 0
        for ref, base, count in refs:
            low, high = max(start, at), min(start + size, at + count)
            if low < high:
                row = base + (half * HALF + j) * count
                parts.append(ref[row + low - at : row + high - at, :])
            at += count
        slabs.append(parts[0] if len(parts) == 1 else jnp.concatenate(parts, axis=0))
    return jnp.concatenate(slabs, axis=1)


def ffn_body(pieces, arrays, sets, fresh, *refs):
    inner, outs = refs[-1], refs[-1 - sets : -1]
    tokens, olds = refs[:sets], refs[sets : 2 * sets]
    held = refs[-1 - sets - arrays : -1 - sets]
    laid = [(held[k], base, count) for k, base, count in pieces]
    total = sum(count for _, _, count in pieces)
    for t in range(sets):
        x = tokens[t][...]
        for s in range(0, total, 256):
            n = min(256, total - s)
            inner[t, :, s : s + n] = gelu(dot_t(x, units(laid, 0, s, n))).astype(bf16)
    down = units(laid, 1, 0, total)
    for t in range(sets):
        for c in range(0, D, 256):
            more = dot(inner[t], down[:, c : c + 256])
            outs[t][:, c : c + 256] = more if fresh else olds[t][:, c : c + 256] + more


def ffn(tokens, olds, arrays, pieces, name):
    sets, rows = len(tokens), tokens[0].shape[0]
    total = sum(count for _, _, count in pieces)
    tail = tuple(tokens) + tuple(olds) + tuple(arrays)
    return pl.pallas_call(
        functools.partial(ffn_body, tuple(pieces), len(arrays), sets, not olds),
        out_shape=(jax.ShapeDtypeStruct((rows, D), f32),) * sets,
        in_specs=vmem(len(tail)),
        out_specs=tuple(vmem(sets)),
        input_output_aliases={sets + t: t for t in range(len(olds))},
        scratch_shapes=[pltpu.VMEM((sets, rows, total), bf16)],
        compiler_params=params(16),
        cost_estimate=LIGHT,
        name=name,
    )(*tail)


def embed_body(length, normed, mine, other, gain, we, out, kept):
    layer = norm_rows(normed[...].astype(f32) + (mine[...] + other[...]), gain[...]).astype(bf16)
    projected = dot(layer, we[...])
    unit = projected * lax.rsqrt(jnp.sum(projected * projected, axis=-1, keepdims=True) + 1e-06)
    slot = lax.broadcasted_iota(jnp.int32, (SEQ, P_SIZE), 0)
    for r in range(normed.shape[0] // SEQ):
        rows = slice(r * SEQ, (r + 1) * SEQ)
        live = jnp.where(slot < length[r], unit[rows], 0.0).astype(bf16)
        out[rows, :] = live
        kept[rows, :] = live


def embed(length, normed, mine, other, gain, we):
    shape = jax.ShapeDtypeStruct((normed.shape[0], P_SIZE), bf16)
    return pl.pallas_call(
        embed_body,
        out_shape=(shape, shape),
        in_specs=[SMEM] + vmem(5),
        out_specs=tuple(vmem(2)),
        compiler_params=params(12),
        cost_estimate=LIGHT,
        name="embed",
    )(length, normed, mine, other, gain.reshape(1, D), we)


def final_body(mine, other, out):
    out[...] = jnp.sum(jnp.maximum(mine[...], other[...]), axis=-1)


def final(mine, other, requests):
    picks = mine.shape[0] // requests
    shape = (requests, picks, mine.shape[1])
    return pl.pallas_call(
        final_body,
        out_shape=jax.ShapeDtypeStruct((requests, picks), f32),
        in_specs=vmem(2),
        out_specs=vmem()[0],
        compiler_params=params(8),
        cost_estimate=LIGHT,
        name="final",
    )(mine.reshape(shape), other.reshape(shape))


def score_body(where, cand, pair, emb, sib, *refs):
    docs, outs, held, sem = refs[:5], refs[5:7], refs[7], refs[8]
    copies = [pltpu.make_async_copy(docs[i], held.at[i], sem.at[i]) for i in range(3)]
    copies += [
        pltpu.make_async_copy(docs[3 + i], held.at[3, 2 * i : 2 * i + 2], sem.at[3 + i]) for i in range(2)
    ]
    for copy in copies:
        copy.start()
    z, x, y, c = where[0], where[1], where[2], where[3]
    local = lax.broadcasted_iota(jnp.int32, (TOKS, LANES), 0)
    pos = jnp.concatenate(
        [local + TOKS * (2 * ((y + d) & 3) + c) for d in AROUND_Y], axis=0
    ).astype(f32)
    row = lax.broadcasted_iota(jnp.int32, (16, LANES), 0)

    def slot(d):
        return jnp.where(d == 0, 0, jnp.where(d == 3, 1, d + 1))

    for copy in copies:
        copy.wait()
    per = cand.shape[0]
    for i in range(2 * per):
        e = cand[i] if i < per else pair[i - per]
        tokens = emb if i < per else sib
        j, req = e & 7, e >> 3
        sz, sx = slot(((req >> 2) - z) & 3), slot(((req & 3) - x) & 3)
        outer = jnp.where(c == 0, sz, sx)
        within = jnp.where(c == 0, sx, sz)
        block = held[outer, within, :, pl.ds(pl.multiple_of(j * TOKS, TOKS), TOKS), :]
        lens = held[outer, within, 0, 8 * TOKS : DOC_ROWS, :].astype(f32)
        limit = jnp.sum(jnp.where(row == j, lens, 0.0), axis=0, keepdims=True)
        r = (i % per) // 8
        sims = dot_t(block.reshape(4 * TOKS, P_SIZE), tokens[r * SEQ : (r + 1) * SEQ, :])
        at = i % per
        outs[i // per][at : at + 1, :] = jnp.max(jnp.where(pos < limit, sims, DEAD), axis=0, keepdims=True)


def score(where, cand, pair, emb, sib, docs):
    total = cand.size
    docs = [d.reshape(-1, 4, DOC_ROWS, P_SIZE) for d in docs]
    return pl.pallas_call(
        score_body,
        out_shape=(jax.ShapeDtypeStruct((total, SEQ), f32),) * 2,
        in_specs=[SMEM] * 3 + vmem(2) + any_spec(5),
        out_specs=tuple(vmem(2)),
        scratch_shapes=[
            pltpu.VMEM((4, 4, 4, DOC_ROWS, P_SIZE), bf16),
            pltpu.SemaphoreType.DMA((5,)),
        ],
        compiler_params=params(8),
        cost_estimate=LIGHT,
        name="score",
    )(where, cand.reshape(-1), pair.reshape(-1), emb, sib, *docs)


def on_device(
    tokens,
    attend_weight,
    output_weight,
    attend_gain,
    up_weight,
    down_weight,
    mlp_gain,
    embed_weight,
    query_length,
    documents,
    document_length,
    candidates,
):
    req, mlp = lax.axis_index("req"), lax.axis_index("mlp")
    z, x, y, c = req // 4, req % 4, mlp // 2, mlp % 2
    where = jnp.stack([z, x, y, c, jnp.where(c == 0, x, z)]).astype(jnp.int32)
    start = first(where, up_weight, down_weight, documents.reshape(-1, P_SIZE), document_length)
    near = [send(start, way) for way in ("y+", "y-", "y2")]
    normed, low, high = attend(
        tokens, attend_weight, output_weight, after(attend_gain, start), query_length, up_weight, down_weight
    )
    pair = send(after(candidates, start), "c")
    near, pair = after((tuple(near), pair), normed)

    whole = [(k, 0, BLOCK) for k in range(3)] + [(3, PART, DOC_ROWS)]
    go = join([*near, start], whole, "join1")
    came = [send(go, way) for way in ("f+", "f-", "f2")]
    pair_normed = send(after(normed, go), "c")
    low_go = after(low, pair_normed)
    low_near = [send(low_go, "y+"), send(low_go, "y-")]
    sets = (normed, pair_normed)
    total = ffn(sets, (), [low, high], [(0, 0, 256), (1, 0, 256)], "ffn1")
    parts = [(i * BLOCK, SLICE) for i in range(3)]
    pieces = [(k, 0, SLICE) for k in range(3)] + [(3,) + p for p in parts]
    total = ffn(sets, total, [*near, came[0]], pieces, "ffn2")
    came, total = after((came, total), *total)
    takes = [(k, at, DOC_ROWS) for k in range(4) for at in [i * BLOCK + PART for i in range(3)] + [3 * BLOCK]]
    docs = join([go, *came], takes, "join2")
    last = [send(docs, way) for way in ("g+", "g-")]
    mid = 128
    low_near = after(tuple(low_near), docs)
    ahead = join([low_near[0]], [(0, k * 256, mid) for k in range(SLABS)], "join5")
    behind = join([low_near[1]], [(0, k * 256 + mid, mid) for k in range(SLABS)], "join6")
    low_far = [send(ahead, "y+"), send(behind, "y-")]
    pieces = [(k,) + p for k in range(2) for p in parts] + [(2, 0, 256), (3, 0, 256)]
    total = ffn(sets, total, [*came[1:], *low_near], pieces, "ffn3")
    parted = halves(*last)
    far_docs = [send(parted[0], "g+"), send(parted[1], "g-")]
    low_far = after(tuple(low_far), *parted)
    rest = [(0, 0, mid), (1, 0, mid)]
    away, = ffn(sets[1:], total[1:], low_far, rest, "ffn4")
    other = send(away, "c")
    mine, = ffn((normed,), total[:1], low_far, rest, "ffn5")
    embedded, kept = embed(query_length, normed, mine, other, mlp_gain, embed_weight)
    sib = send(kept, "c")
    best, best_pair = score(where, candidates, pair, kept, sib, [docs, *last, *far_docs])
    scores = final(best, send(best_pair, "c"), candidates.shape[0])
    return (embedded, scores)


def solution(mesh):
    return jax.shard_map(
        on_device,
        mesh=mesh,
        in_specs=(
            P(("req", "mlp"), None),
            P(),
            P(),
            P(),
            P(None, "mlp"),
            P(None, "mlp"),
            P(),
            P(),
            P(("req", "mlp")),
            P("req", "mlp", None),
            P("req"),
            P(("req", "mlp"), None),
        ),
        out_specs=(P(("req", "mlp"), None), P(("req", "mlp"), None)),
        check_vma=False,
    )
```

```python
import functools

import jax
import jax.numpy as jnp
from jax import lax
from jax.experimental import pallas as pl
from jax.experimental.pallas import tpu as pltpu
from jax.sharding import PartitionSpec as P

D = 1024
HEADS = 16
HD = 64
P_SIZE = 128
SEQ = 128
LANES = 128
SLABS = 2 * D // LANES
HALF = SLABS // 2
TOKS = 32
DOC_ROWS = 272
SLICE = 64
PART = SLABS * SLICE
BLOCK = PART + DOC_ROWS
AROUND = (0, 3, 1, 2)
AROUND_Y = (3, 1, 2, 0)
DEAD = -1e30
f32 = jnp.float32
bf16 = jnp.bfloat16


def dot(a, b):
    return jnp.dot(a, b, preferred_element_type=f32)


def dot_t(a, b):
    return lax.dot_general(a, b, (((1,), (1,)), ((), ())), preferred_element_type=f32)


def norm_rows(values, scaling):
    average = jnp.mean(values, axis=-1, keepdims=True)
    centred = values - average
    variance = jnp.mean(centred * centred, axis=-1, keepdims=True)
    return centred * lax.rsqrt(variance + 1e-05) * scaling


def gelu(x):
    return 0.5 * x * (1.0 + lax.erf(x * (0.5 ** 0.5)))


LIGHT = pl.CostEstimate(flops=1, transcendentals=0, bytes_accessed=1)


def params(mib):
    return pltpu.CompilerParams(vmem_limit_bytes=mib * 1024 * 1024)


def vmem(n=1):
    return [pl.BlockSpec(memory_space=pltpu.VMEM)] * n


def place(z, x, y, c):
    return ((z % 4) * 4 + x % 4) * 8 + (y % 4) * 2 + c % 2


def shift(move):
    return [
        (place(z, x, y, c), place(*move(z, x, y, c)))
        for z in range(4)
        for x in range(4)
        for y in range(4)
        for c in range(2)
    ]


def along_y(d):
    return shift(lambda z, x, y, c: (z, x, y + d, c))


def crossed(d, first):
    return shift(lambda z, x, y, c: (z, x + d, y, c) if c == first else (z + d, x, y, c))


STEPS = {"y+": along_y(1), "y-": along_y(-1), "y2": along_y(2)}
for name, d in (("+", 1), ("-", -1), ("2", 2)):
    STEPS["f" + name] = crossed(d, 0)
    STEPS["g" + name] = crossed(d, 1)
STEPS["c"] = shift(lambda z, x, y, c: (z, x, y, c + 1))


def send(value, way):
    return lax.ppermute(value, ("req", "mlp"), STEPS[way])


def after(value, *first):
    return lax.optimization_barrier((value, first))[0]


def any_spec(n=1):
    return [pl.BlockSpec(memory_space=pl.ANY)] * n


def pinned(*arrays):
    return [pltpu.with_memory_space_constraint(a, pltpu.HBM) for a in arrays]


def hbm(n=1):
    return [pl.BlockSpec(memory_space=pltpu.HBM)] * n


SMEM = pl.BlockSpec(memory_space=pltpu.SMEM)


def first_body(where, up, down, docs, lengths, qkv, out, query, held, turned, limits, sems):
    index = where[4]
    lanes = pl.ds(pl.multiple_of(256 + (index >> 1) * LANES, LANES), LANES)
    copies = [pltpu.make_async_copy(w.at[:, lanes], held.at[k], sems.at[k]) for k, w in enumerate((up, down))]
    tokens = DOC_ROWS - 16
    copies.append(pltpu.make_async_copy(docs, out.at[PART : PART + tokens], sems.at[2]))
    copies.append(pltpu.make_async_copy(lengths, limits, sems.at[3]))
    copies.append(pltpu.make_async_copy(qkv.at[:, :D], query, sems.at[4]))
    for copy in copies:
        copy.start()
    start = pl.multiple_of((index & 1) * SLICE, SLICE)
    for k in range(2):
        copies[k].wait()
        for j in range(HALF):
            slab = k * HALF + j
            turned[slab] = held[k, j * LANES : (j + 1) * LANES, :].T
            out[slab * SLICE : (slab + 1) * SLICE, :] = turned[slab, pl.ds(start, SLICE), :]
    copies[3].wait()
    row = lax.broadcasted_iota(jnp.int32, (16, LANES), 0)
    limit = jnp.zeros((16, LANES), f32)
    for j in range(8):
        limit = jnp.where(row == j, limits[j].astype(f32), limit)
    out[PART + tokens : BLOCK, :] = limit.astype(bf16)
    copies[2].wait()
    copies[4].wait()


def first(where, up, down, docs, lengths, qkv):
    return pl.pallas_call(
        first_body,
        out_shape=(jax.ShapeDtypeStruct((BLOCK, LANES), bf16), jax.ShapeDtypeStruct((D, D), bf16)),
        in_specs=[SMEM] + hbm(5),
        out_specs=tuple(vmem(2)),
        scratch_shapes=[
            pltpu.VMEM((2, D, LANES), bf16),
            pltpu.VMEM((SLABS, LANES, LANES), bf16),
            pltpu.SMEM((8,), jnp.int32),
            pltpu.SemaphoreType.DMA((5,)),
        ],
        compiler_params=params(8),
        cost_estimate=LIGHT,
        name="first",
    )(where, *pinned(up, down, docs, lengths, qkv))


def join_body(takes, *refs):
    out, at = refs[-1], 0
    for k, start, size in takes:
        out[at : at + size, :] = refs[k][start : start + size, :]
        at += size


def join(arrays, takes, name):
    return pl.pallas_call(
        functools.partial(join_body, takes),
        out_shape=jax.ShapeDtypeStruct((sum(t[2] for t in takes), LANES), bf16),
        in_specs=vmem(len(arrays)),
        out_specs=vmem()[0],
        compiler_params=params(16),
        cost_estimate=LIGHT,
        name=name,
    )(*arrays)


def norm_into(out, values, gain, block=32):
    for at in range(0, out.shape[0], block):
        rows = slice(at, at + block)
        out[rows, :] = norm_rows(values(rows), gain).astype(bf16)


def attend_body(
    length, qkv, wo_hbm, up, down, tok, query, gain, out, low_out, high_out, packed, context, held, wo, wide, added, sems
):
    rows_all = tok.shape[0]
    step = 512
    sources = [(qkv.at[:, D + c : D + c + step], held.at[:, c : c + step]) for c in range(0, 2 * D, step)]
    sources += [(up, wide.at[0]), (down, wide.at[1]), (wo_hbm, wo)]
    copies = [pltpu.make_async_copy(source, target, sems.at[i]) for i, (source, target) in enumerate(sources)]
    for copy in copies[:4]:
        copy.start()
    packed[:, :D] = dot(tok[...], query[...]).astype(bf16)
    for copy in copies[4:]:
        copy.start()
    for i in range(4):
        copies[i].wait()
        columns = slice(i * step, (i + 1) * step)
        packed[:, D + i * step : D + (i + 1) * step] = dot(tok[...], held[:, columns]).astype(bf16)
    for k in range(2):
        copies[4 + k].wait()
        for j in range(HALF):
            rows = slice(j * LANES, (j + 1) * LANES)
            low_out[k * HALF + j] = wide[k, rows, :256].T
            high_out[k * HALF + j] = wide[k, rows, 256:].T
    lane = lax.broadcasted_iota(jnp.int32, (2 * SEQ, LANES), 1)
    low = lax.broadcasted_iota(jnp.int32, (SEQ, LANES), 1) < HD

    def request(r, carry):
        rows = pl.ds(pl.multiple_of(r * SEQ, SEQ), SEQ)
        live = lane < length[r]
        for p in range(HEADS // 2):
            at = p * LANES
            q = packed[rows, at : at + LANES]
            k = packed[rows, D + at : D + at + LANES]
            v = packed[rows, 2 * D + at : 2 * D + at + LANES]
            zero = jnp.zeros_like(q)
            both = jnp.concatenate([jnp.where(low, q, zero), jnp.where(low, zero, q)], axis=0)
            logits = jnp.where(live, dot_t(both, k) * HD ** (-0.5), DEAD)
            weights = jnp.exp(logits - jnp.max(logits, axis=-1, keepdims=True))
            probs = (weights * (1.0 / jnp.sum(weights, axis=-1, keepdims=True))).astype(bf16)
            ctx = dot(probs, v)
            context[rows, at : at + LANES] = jnp.where(low, ctx[:SEQ], ctx[SEQ:]).astype(bf16)
        return carry

    lax.fori_loop(0, rows_all // SEQ, request, 0)
    copies[6].wait()
    added[...] = dot(context[...], wo[...])
    norm_into(out, lambda rows: tok[rows, :].astype(f32) + added[rows, :], gain[...])


def attend(tokens, qkv, query, wo, gain, length, up, down):
    rows = tokens.shape[0]
    piece = jax.ShapeDtypeStruct((SLABS, 256, LANES), bf16)
    normed, low, high = pl.pallas_call(
        attend_body,
        out_shape=(jax.ShapeDtypeStruct((rows, D), bf16), piece, piece),
        in_specs=[SMEM] + hbm(4) + vmem(3),
        out_specs=tuple(vmem(3)),
        scratch_shapes=[
            pltpu.VMEM((rows, 3 * D), bf16),
            pltpu.VMEM((rows, D), bf16),
            pltpu.VMEM((D, 2 * D), bf16),
            pltpu.VMEM((D, D), bf16),
            pltpu.VMEM((2, D, 512), bf16),
            pltpu.VMEM((rows, D), f32),
            pltpu.SemaphoreType.DMA((7,)),
        ],
        compiler_params=params(28),
        cost_estimate=LIGHT,
        name="attend",
    )(length, *pinned(qkv, wo, up, down), tokens, query, gain.reshape(1, D))
    return normed, low.reshape(-1, LANES), high.reshape(-1, LANES)


def halves_body(plus, minus, low, high, sems):
    rows = low.shape[0]
    copies = [
        pltpu.make_async_copy(plus.at[:rows], low, sems.at[0]),
        pltpu.make_async_copy(minus.at[rows:], high, sems.at[1]),
    ]
    for copy in copies:
        copy.start()
    for copy in copies:
        copy.wait()


def halves(plus, minus):
    half = jax.ShapeDtypeStruct((plus.shape[0] // 2, LANES), bf16)
    return pl.pallas_call(
        halves_body,
        out_shape=(half, half),
        in_specs=any_spec(2),
        out_specs=tuple(any_spec(2)),
        scratch_shapes=[pltpu.SemaphoreType.DMA((2,))],
        compiler_params=params(8),
        cost_estimate=LIGHT,
        name="halves",
    )(plus, minus)


def units(refs, half, start, size):
    slabs = []
    for j in range(HALF):
        parts, at = [], 0
        for ref, base, count in refs:
            low, high = max(start, at), min(start + size, at + count)
            if low < high:
                row = base + (half * HALF + j) * count
                parts.append(ref[row + low - at : row + high - at, :])
            at += count
        slabs.append(parts[0] if len(parts) == 1 else jnp.concatenate(parts, axis=0))
    return jnp.concatenate(slabs, axis=1)


def ffn_body(pieces, arrays, sets, fresh, *refs):
    inner, outs = refs[-1], refs[-1 - sets : -1]
    tokens, olds = refs[:sets], refs[sets : 2 * sets]
    held = refs[-1 - sets - arrays : -1 - sets]
    laid = [(held[k], base, count) for k, base, count in pieces]
    total = sum(count for _, _, count in pieces)
    for t in range(sets):
        x = tokens[t][...]
        for s in range(0, total, 256):
            n = min(256, total - s)
            inner[t, :, s : s + n] = gelu(dot_t(x, units(laid, 0, s, n))).astype(bf16)
    down = units(laid, 1, 0, total)
    for t in range(sets):
        for c in range(0, D, 256):
            more = dot(inner[t], down[:, c : c + 256])
            outs[t][:, c : c + 256] = more if fresh else olds[t][:, c : c + 256] + more


def ffn(tokens, olds, arrays, pieces, name):
    sets, rows = len(tokens), tokens[0].shape[0]
    total = sum(count for _, _, count in pieces)
    tail = tuple(tokens) + tuple(olds) + tuple(arrays)
    return pl.pallas_call(
        functools.partial(ffn_body, tuple(pieces), len(arrays), sets, not olds),
        out_shape=(jax.ShapeDtypeStruct((rows, D), f32),) * sets,
        in_specs=vmem(len(tail)),
        out_specs=tuple(vmem(sets)),
        input_output_aliases={sets + t: t for t in range(len(olds))},
        scratch_shapes=[pltpu.VMEM((sets, rows, total), bf16)],
        compiler_params=params(16),
        cost_estimate=LIGHT,
        name=name,
    )(*tail)


def embed_body(length, normed, mine, other, gain, we, out, kept, layer):
    norm_into(
        layer, lambda rows: normed[rows, :].astype(f32) + (mine[rows, :] + other[rows, :]), gain[...]
    )
    projected = dot(layer[...], we[...])
    unit = projected * lax.rsqrt(jnp.sum(projected * projected, axis=-1, keepdims=True) + 1e-06)
    slot = lax.broadcasted_iota(jnp.int32, (SEQ, P_SIZE), 0)
    for r in range(normed.shape[0] // SEQ):
        rows = slice(r * SEQ, (r + 1) * SEQ)
        live = jnp.where(slot < length[r], unit[rows], 0.0).astype(bf16)
        out[rows, :] = live
        kept[rows, :] = live


def embed(length, normed, mine, other, gain, we):
    shape = jax.ShapeDtypeStruct((normed.shape[0], P_SIZE), bf16)
    return pl.pallas_call(
        embed_body,
        out_shape=(shape, shape),
        in_specs=[SMEM] + vmem(5),
        out_specs=tuple(vmem(2)),
        scratch_shapes=[pltpu.VMEM(normed.shape, bf16)],
        compiler_params=params(12),
        cost_estimate=LIGHT,
        name="embed",
    )(length, normed, mine, other, gain.reshape(1, D), we)


def final_body(mine, other, out):
    out[...] = jnp.sum(jnp.maximum(mine[...], other[...]), axis=-1)


def final(mine, other, requests):
    picks = mine.shape[0] // requests
    shape = (requests, picks, mine.shape[1])
    return pl.pallas_call(
        final_body,
        out_shape=jax.ShapeDtypeStruct((requests, picks), f32),
        in_specs=vmem(2),
        out_specs=vmem()[0],
        compiler_params=params(8),
        cost_estimate=LIGHT,
        name="final",
    )(mine.reshape(shape), other.reshape(shape))


def score_body(where, cand, pair, emb, sib, *refs):
    docs, outs, held, sem = refs[:5], refs[5:7], refs[7], refs[8]
    copies = [pltpu.make_async_copy(docs[i], held.at[i], sem.at[i]) for i in range(3)]
    copies += [
        pltpu.make_async_copy(docs[3 + i], held.at[3, 2 * i : 2 * i + 2], sem.at[3 + i]) for i in range(2)
    ]
    for copy in copies:
        copy.start()
    z, x, y, c = where[0], where[1], where[2], where[3]
    local = lax.broadcasted_iota(jnp.int32, (TOKS, LANES), 0)
    pos = jnp.concatenate(
        [local + TOKS * (2 * ((y + d) & 3) + c) for d in AROUND_Y], axis=0
    ).astype(f32)
    row = lax.broadcasted_iota(jnp.int32, (16, LANES), 0)

    def slot(d):
        return jnp.where(d == 0, 0, jnp.where(d == 3, 1, d + 1))

    for copy in copies:
        copy.wait()
    per = cand.shape[0]
    picks = 8
    for first_pick in range(0, 2 * per, picks):
        blocks, limits = [], []
        for i in range(first_pick, first_pick + picks):
            e = cand[i] if i < per else pair[i - per]
            j, req = e & 7, e >> 3
            sz, sx = slot(((req >> 2) - z) & 3), slot(((req & 3) - x) & 3)
            outer = jnp.where(c == 0, sz, sx)
            within = jnp.where(c == 0, sx, sz)
            block = held[outer, within, :, pl.ds(pl.multiple_of(j * TOKS, TOKS), TOKS), :]
            blocks.append(block.reshape(4 * TOKS, P_SIZE))
            lens = held[outer, within, 0, 8 * TOKS : DOC_ROWS, :].astype(f32)
            limits.append(jnp.sum(jnp.where(row == j, lens, 0.0), axis=0, keepdims=True))
        at = first_pick % per
        tokens = emb if first_pick < per else sib
        r = at // picks
        sims = dot_t(jnp.concatenate(blocks, axis=0), tokens[r * SEQ : (r + 1) * SEQ, :])
        for k in range(picks):
            some = jnp.where(pos < limits[k], sims[k * 4 * TOKS : (k + 1) * 4 * TOKS], DEAD)
            outs[first_pick // per][at + k : at + k + 1, :] = jnp.max(some, axis=0, keepdims=True)


def score(where, cand, pair, emb, sib, docs):
    total = cand.size
    docs = [d.reshape(-1, 4, DOC_ROWS, P_SIZE) for d in docs]
    return pl.pallas_call(
        score_body,
        out_shape=(jax.ShapeDtypeStruct((total, SEQ), f32),) * 2,
        in_specs=[SMEM] * 3 + vmem(2) + any_spec(5),
        out_specs=tuple(vmem(2)),
        scratch_shapes=[
            pltpu.VMEM((4, 4, 4, DOC_ROWS, P_SIZE), bf16),
            pltpu.SemaphoreType.DMA((5,)),
        ],
        compiler_params=params(8),
        cost_estimate=LIGHT,
        name="score",
    )(where, cand.reshape(-1), pair.reshape(-1), emb, sib, *docs)


def on_device(
    tokens,
    attend_weight,
    output_weight,
    attend_gain,
    up_weight,
    down_weight,
    mlp_gain,
    embed_weight,
    query_length,
    documents,
    document_length,
    candidates,
):
    req, mlp = lax.axis_index("req"), lax.axis_index("mlp")
    z, x, y, c = req // 4, req % 4, mlp // 2, mlp % 2
    where = jnp.stack([z, x, y, c, jnp.where(c == 0, x, z)]).astype(jnp.int32)
    start, query = first(
        where, up_weight, down_weight, documents.reshape(-1, P_SIZE), document_length, attend_weight
    )
    near = [send(start, way) for way in ("y+", "y-", "y2")]
    normed, low, high = attend(
        tokens, attend_weight, query, output_weight, attend_gain, query_length, up_weight, down_weight
    )
    pair = send(after(candidates, start), "c")
    near, pair = after((tuple(near), pair), normed)

    whole = [(k, 0, BLOCK) for k in range(3)] + [(3, PART, DOC_ROWS)]
    go = join([*near, start], whole, "join1")
    came = [send(go, way) for way in ("f+", "f-", "f2")]
    pair_normed = send(after(normed, go), "c")
    low_go = after(low, pair_normed)
    low_near = [send(low_go, "y+"), send(low_go, "y-")]
    sets = (normed, pair_normed)
    total = ffn(sets, (), [low, high], [(0, 0, 256), (1, 0, 256)], "ffn1")
    parts = [(i * BLOCK, SLICE) for i in range(3)]
    pieces = [(k, 0, SLICE) for k in range(3)] + [(3,) + p for p in parts]
    total = ffn(sets, total, [*near, came[0]], pieces, "ffn2")
    came, total = after((came, total), *total)
    takes = [(k, at, DOC_ROWS) for k in range(4) for at in [i * BLOCK + PART for i in range(3)] + [3 * BLOCK]]
    docs = join([go, *came], takes, "join2")
    last = [send(docs, way) for way in ("g+", "g-")]
    mid = 128
    low_near = after(tuple(low_near), docs)
    ahead = join([low_near[0]], [(0, k * 256, mid) for k in range(SLABS)], "join5")
    behind = join([low_near[1]], [(0, k * 256 + mid, mid) for k in range(SLABS)], "join6")
    low_far = [send(ahead, "y+"), send(behind, "y-")]
    pieces = [(k,) + p for k in range(2) for p in parts] + [(2, 0, 256), (3, 0, 256)]
    total = ffn(sets, total, [*came[1:], *low_near], pieces, "ffn3")
    parted = halves(*last)
    far_docs = [send(parted[0], "g+"), send(parted[1], "g-")]
    low_far = after(tuple(low_far), *parted)
    rest = [(0, 0, mid), (1, 0, mid)]
    away, = ffn(sets[1:], total[1:], low_far, rest, "ffn4")
    other = send(away, "c")
    mine, = ffn((normed,), total[:1], low_far, rest, "ffn5")
    embedded, kept = embed(query_length, normed, mine, other, mlp_gain, embed_weight)
    sib = send(kept, "c")
    best, best_pair = score(where, candidates, pair, kept, sib, [docs, *last, *far_docs])
    scores = final(best, send(best_pair, "c"), candidates.shape[0])
    return (embedded, scores)


def solution(mesh):
    return jax.shard_map(
        on_device,
        mesh=mesh,
        in_specs=(
            P(("req", "mlp"), None),
            P(),
            P(),
            P(),
            P(None, "mlp"),
            P(None, "mlp"),
            P(),
            P(),
            P(("req", "mlp")),
            P("req", "mlp", None),
            P("req"),
            P(("req", "mlp"), None),
        ),
        out_specs=(P(("req", "mlp"), None), P(("req", "mlp"), None)),
        check_vma=False,
    )
```

```python
import functools

import jax
import jax.numpy as jnp
from jax import lax
from jax.experimental import pallas as pl
from jax.experimental.pallas import tpu as pltpu
from jax.sharding import PartitionSpec as P

D = 1024
HEADS = 16
HD = 64
P_SIZE = 128
SEQ = 128
LANES = 128
SLABS = 2 * D // LANES
HALF = SLABS // 2
TOKS = 32
DOC_ROWS = 272
SLICE = 64
PART = SLABS * SLICE
BLOCK = PART + DOC_ROWS
AROUND = (0, 3, 1, 2)
AROUND_Y = (3, 1, 2, 0)
DEAD = -1e30
f32 = jnp.float32
bf16 = jnp.bfloat16


def dot(a, b):
    return jnp.dot(a, b, preferred_element_type=f32)


def dot_t(a, b):
    return lax.dot_general(a, b, (((1,), (1,)), ((), ())), preferred_element_type=f32)


def norm_rows(values, scaling):
    average = jnp.mean(values, axis=-1, keepdims=True)
    centred = values - average
    variance = jnp.mean(centred * centred, axis=-1, keepdims=True)
    return centred * lax.rsqrt(variance + 1e-05) * scaling


def gelu(x):
    return 0.5 * x * (1.0 + lax.erf(x * (0.5 ** 0.5)))


LIGHT = pl.CostEstimate(flops=1, transcendentals=0, bytes_accessed=1)


def params(mib):
    return pltpu.CompilerParams(vmem_limit_bytes=mib * 1024 * 1024)


def vmem(n=1):
    return [pl.BlockSpec(memory_space=pltpu.VMEM)] * n


def place(z, x, y, c):
    return ((z % 4) * 4 + x % 4) * 8 + (y % 4) * 2 + c % 2


def shift(move):
    return [
        (place(z, x, y, c), place(*move(z, x, y, c)))
        for z in range(4)
        for x in range(4)
        for y in range(4)
        for c in range(2)
    ]


def along_y(d):
    return shift(lambda z, x, y, c: (z, x, y + d, c))


def crossed(d, first):
    return shift(lambda z, x, y, c: (z, x + d, y, c) if c == first else (z + d, x, y, c))


STEPS = {"y+": along_y(1), "y-": along_y(-1), "y2": along_y(2)}
for name, d in (("+", 1), ("-", -1), ("2", 2)):
    STEPS["f" + name] = crossed(d, 0)
    STEPS["g" + name] = crossed(d, 1)
STEPS["c"] = shift(lambda z, x, y, c: (z, x, y, c + 1))


def send(value, way):
    return lax.ppermute(value, ("req", "mlp"), STEPS[way])


def after(value, *first):
    return lax.optimization_barrier((value, first))[0]


def any_spec(n=1):
    return [pl.BlockSpec(memory_space=pl.ANY)] * n


def pinned(*arrays):
    return [pltpu.with_memory_space_constraint(a, pltpu.HBM) for a in arrays]


def hbm(n=1):
    return [pl.BlockSpec(memory_space=pltpu.HBM)] * n


SMEM = pl.BlockSpec(memory_space=pltpu.SMEM)


def first_body(where, up, down, docs, lengths, qkv, out, query, held, turned, limits, sems):
    index = where[4]
    lanes = pl.ds(pl.multiple_of(256 + (index >> 1) * LANES, LANES), LANES)
    copies = [pltpu.make_async_copy(w.at[:, lanes], held.at[k], sems.at[k]) for k, w in enumerate((up, down))]
    tokens = DOC_ROWS - 16
    copies.append(pltpu.make_async_copy(docs, out.at[PART : PART + tokens], sems.at[2]))
    copies.append(pltpu.make_async_copy(lengths, limits, sems.at[3]))
    copies.append(pltpu.make_async_copy(qkv.at[:, :D], query, sems.at[4]))
    for copy in copies:
        copy.start()
    start = pl.multiple_of((index & 1) * SLICE, SLICE)
    for k in range(2):
        copies[k].wait()
        for j in range(HALF):
            slab = k * HALF + j
            turned[slab] = held[k, j * LANES : (j + 1) * LANES, :].T
            out[slab * SLICE : (slab + 1) * SLICE, :] = turned[slab, pl.ds(start, SLICE), :]
    copies[3].wait()
    row = lax.broadcasted_iota(jnp.int32, (16, LANES), 0)
    limit = jnp.zeros((16, LANES), f32)
    for j in range(8):
        limit = jnp.where(row == j, limits[j].astype(f32), limit)
    out[PART + tokens : BLOCK, :] = limit.astype(bf16)
    copies[2].wait()
    copies[4].wait()


def first(where, up, down, docs, lengths, qkv):
    return pl.pallas_call(
        first_body,
        out_shape=(jax.ShapeDtypeStruct((BLOCK, LANES), bf16), jax.ShapeDtypeStruct((D, D), bf16)),
        in_specs=[SMEM] + hbm(5),
        out_specs=tuple(vmem(2)),
        scratch_shapes=[
            pltpu.VMEM((2, D, LANES), bf16),
            pltpu.VMEM((SLABS, LANES, LANES), bf16),
            pltpu.SMEM((8,), jnp.int32),
            pltpu.SemaphoreType.DMA((5,)),
        ],
        compiler_params=params(8),
        cost_estimate=LIGHT,
        name="first",
    )(where, *pinned(up, down, docs, lengths, qkv))


def join_body(takes, *refs):
    out, at = refs[-1], 0
    for k, start, size in takes:
        out[at : at + size, :] = refs[k][start : start + size, :]
        at += size


def join(arrays, takes, name):
    return pl.pallas_call(
        functools.partial(join_body, takes),
        out_shape=jax.ShapeDtypeStruct((sum(t[2] for t in takes), LANES), bf16),
        in_specs=vmem(len(arrays)),
        out_specs=vmem()[0],
        compiler_params=params(16),
        cost_estimate=LIGHT,
        name=name,
    )(*arrays)


def norm_into(out, values, gain, block=32):
    for at in range(0, out.shape[0], block):
        rows = slice(at, at + block)
        out[rows, :] = norm_rows(values(rows), gain).astype(bf16)


def attend_body(
    length, qkv, wo_hbm, up, down, tok, query, gain, out, low_out, high_out, packed, context, held, wo, wide, added, sems
):
    rows_all = tok.shape[0]
    step = 512
    sources = [(qkv.at[:, D + c : D + c + step], held.at[:, c : c + step]) for c in range(0, 2 * D, step)]
    sources += [(up, wide.at[0]), (down, wide.at[1]), (wo_hbm, wo)]
    copies = [pltpu.make_async_copy(source, target, sems.at[i]) for i, (source, target) in enumerate(sources)]
    for copy in copies[:4]:
        copy.start()
    packed[:, :D] = dot(tok[...], query[...]).astype(bf16)
    for copy in copies[4:]:
        copy.start()
    for i in range(4):
        copies[i].wait()
        columns = slice(i * step, (i + 1) * step)
        packed[:, D + i * step : D + (i + 1) * step] = dot(tok[...], held[:, columns]).astype(bf16)
    for k in range(2):
        copies[4 + k].wait()
        for j in range(HALF):
            rows = slice(j * LANES, (j + 1) * LANES)
            low_out[k * HALF + j] = wide[k, rows, :256].T
            high_out[k * HALF + j] = wide[k, rows, 256:].T
    lane = lax.broadcasted_iota(jnp.int32, (2 * SEQ, LANES), 1)
    low = lax.broadcasted_iota(jnp.int32, (SEQ, LANES), 1) < HD

    def request(r, carry):
        rows = pl.ds(pl.multiple_of(r * SEQ, SEQ), SEQ)
        live = lane < length[r]
        for p in range(HEADS // 2):
            at = p * LANES
            q = packed[rows, at : at + LANES]
            k = packed[rows, D + at : D + at + LANES]
            v = packed[rows, 2 * D + at : 2 * D + at + LANES]
            zero = jnp.zeros_like(q)
            both = jnp.concatenate([jnp.where(low, q, zero), jnp.where(low, zero, q)], axis=0)
            logits = jnp.where(live, dot_t(both, k) * HD ** (-0.5), DEAD)
            weights = jnp.exp(logits - jnp.max(logits, axis=-1, keepdims=True))
            probs = (weights * (1.0 / jnp.sum(weights, axis=-1, keepdims=True))).astype(bf16)
            ctx = dot(probs, v)
            context[rows, at : at + LANES] = jnp.where(low, ctx[:SEQ], ctx[SEQ:]).astype(bf16)
        return carry

    lax.fori_loop(0, rows_all // SEQ, request, 0)
    copies[6].wait()
    added[...] = dot(context[...], wo[...])
    norm_into(out, lambda rows: tok[rows, :].astype(f32) + added[rows, :], gain[...])


def attend(tokens, qkv, query, wo, gain, length, up, down):
    rows = tokens.shape[0]
    piece = jax.ShapeDtypeStruct((SLABS, 256, LANES), bf16)
    normed, low, high = pl.pallas_call(
        attend_body,
        out_shape=(jax.ShapeDtypeStruct((rows, D), bf16), piece, piece),
        in_specs=[SMEM] + hbm(4) + vmem(3),
        out_specs=tuple(vmem(3)),
        scratch_shapes=[
            pltpu.VMEM((rows, 3 * D), bf16),
            pltpu.VMEM((rows, D), bf16),
            pltpu.VMEM((D, 2 * D), bf16),
            pltpu.VMEM((D, D), bf16),
            pltpu.VMEM((2, D, 512), bf16),
            pltpu.VMEM((rows, D), f32),
            pltpu.SemaphoreType.DMA((7,)),
        ],
        compiler_params=params(28),
        cost_estimate=LIGHT,
        name="attend",
    )(length, *pinned(qkv, wo, up, down), tokens, query, gain.reshape(1, D))
    return normed, low.reshape(-1, LANES), high.reshape(-1, LANES)


def units(refs, half, start, size):
    slabs = []
    for j in range(HALF):
        parts, at = [], 0
        for ref, base, count in refs:
            low, high = max(start, at), min(start + size, at + count)
            if low < high:
                row = base + (half * HALF + j) * count
                parts.append(ref[row + low - at : row + high - at, :])
            at += count
        slabs.append(parts[0] if len(parts) == 1 else jnp.concatenate(parts, axis=0))
    return jnp.concatenate(slabs, axis=1)


def ffn_body(pieces, arrays, sets, fresh, split, *refs):
    inner, outs = refs[-1], refs[-1 - sets * split : -1]
    tokens, olds = refs[:sets], refs[sets : 2 * sets]
    held = refs[-1 - sets * split - arrays : -1 - sets * split]
    laid = [(held[k], base, count) for k, base, count in pieces]
    total = sum(count for _, _, count in pieces)
    for t in range(sets):
        x = tokens[t][...]
        for s in range(0, total, 256):
            n = min(256, total - s)
            inner[t, :, s : s + n] = gelu(dot_t(x, units(laid, 0, s, n))).astype(bf16)
    down = units(laid, 1, 0, total)
    for t in range(sets):
        for c in range(0, D, 256):
            more = dot(inner[t], down[:, c : c + 256])
            more = more if fresh else olds[t][:, c : c + 256] + more
            rows = more.shape[0] // split
            for k in range(split):
                outs[t * split + k][:, c : c + 256] = more[k * rows : (k + 1) * rows]


def ffn(tokens, olds, arrays, pieces, name, split=1):
    sets, rows = len(tokens), tokens[0].shape[0]
    total = sum(count for _, _, count in pieces)
    tail = tuple(tokens) + tuple(olds) + tuple(arrays)
    return pl.pallas_call(
        functools.partial(ffn_body, tuple(pieces), len(arrays), sets, not olds, split),
        out_shape=(jax.ShapeDtypeStruct((rows // split, D), f32),) * (sets * split),
        in_specs=vmem(len(tail)),
        out_specs=tuple(vmem(sets * split)),
        input_output_aliases={sets + t: t for t in range(len(olds))} if split == 1 else {},
        scratch_shapes=[pltpu.VMEM((sets, rows, total), bf16)],
        compiler_params=params(16),
        cost_estimate=LIGHT,
        name=name,
    )(*tail)


def embed_body(length, normed, mine, other0, other1, gain, we, out, kept, layer):
    half = other0.shape[0]
    for k, other in enumerate((other0, other1)):
        norm_into(
            layer.at[k * half : (k + 1) * half],
            lambda rows: normed[k * half + rows.start : k * half + rows.stop, :].astype(f32)
            + (mine[k * half + rows.start : k * half + rows.stop, :] + other[rows, :]),
            gain[...],
        )
    projected = dot(layer[...], we[...])
    unit = projected * lax.rsqrt(jnp.sum(projected * projected, axis=-1, keepdims=True) + 1e-06)
    slot = lax.broadcasted_iota(jnp.int32, (SEQ, P_SIZE), 0)
    for r in range(normed.shape[0] // SEQ):
        rows = slice(r * SEQ, (r + 1) * SEQ)
        live = jnp.where(slot < length[r], unit[rows], 0.0).astype(bf16)
        out[rows, :] = live
        kept[rows, :] = live


def embed(length, normed, mine, other0, other1, gain, we):
    shape = jax.ShapeDtypeStruct((normed.shape[0], P_SIZE), bf16)
    return pl.pallas_call(
        embed_body,
        out_shape=(shape, shape),
        in_specs=[SMEM] + vmem(6),
        out_specs=tuple(vmem(2)),
        scratch_shapes=[pltpu.VMEM(normed.shape, bf16)],
        compiler_params=params(12),
        cost_estimate=LIGHT,
        name="embed",
    )(length, normed, mine, other0, other1, gain.reshape(1, D), we)


def final_body(mine, other, out):
    out[...] = jnp.sum(jnp.maximum(mine[...], other[...]), axis=-1)


def final(mine, other, requests):
    picks = mine.shape[0] // requests
    shape = (requests, picks, mine.shape[1])
    return pl.pallas_call(
        final_body,
        out_shape=jax.ShapeDtypeStruct((requests, picks), f32),
        in_specs=vmem(2),
        out_specs=vmem()[0],
        compiler_params=params(8),
        cost_estimate=LIGHT,
        name="final",
    )(mine.reshape(shape), other.reshape(shape))


def score_body(where, cand, pair, emb, sib, *refs):
    docs, outs, held, sem = refs[:4], refs[4:6], refs[6], refs[7]
    copies = [pltpu.make_async_copy(docs[i], held.at[i], sem.at[i]) for i in range(4)]
    for copy in copies:
        copy.start()
    z, x, y, c = where[0], where[1], where[2], where[3]
    local = lax.broadcasted_iota(jnp.int32, (TOKS, LANES), 0)
    pos = jnp.concatenate(
        [local + TOKS * (2 * ((y + d) & 3) + c) for d in AROUND_Y], axis=0
    ).astype(f32)
    row = lax.broadcasted_iota(jnp.int32, (16, LANES), 0)

    def slot(d):
        return jnp.where(d == 0, 0, jnp.where(d == 3, 1, d + 1))

    for copy in copies:
        copy.wait()
    per = cand.shape[0]
    picks = 8
    for first_pick in range(0, 2 * per, picks):
        blocks, limits = [], []
        for i in range(first_pick, first_pick + picks):
            e = cand[i] if i < per else pair[i - per]
            j, req = e & 7, e >> 3
            sz, sx = slot(((req >> 2) - z) & 3), slot(((req & 3) - x) & 3)
            outer = jnp.where(c == 0, sz, sx)
            within = jnp.where(c == 0, sx, sz)
            block = held[outer, within, :, pl.ds(pl.multiple_of(j * TOKS, TOKS), TOKS), :]
            blocks.append(block.reshape(4 * TOKS, P_SIZE))
            lens = held[outer, within, 0, 8 * TOKS : DOC_ROWS, :].astype(f32)
            limits.append(jnp.sum(jnp.where(row == j, lens, 0.0), axis=0, keepdims=True))
        at = first_pick % per
        tokens = emb if first_pick < per else sib
        r = at // picks
        sims = dot_t(jnp.concatenate(blocks, axis=0), tokens[r * SEQ : (r + 1) * SEQ, :])
        for k in range(picks):
            some = jnp.where(pos < limits[k], sims[k * 4 * TOKS : (k + 1) * 4 * TOKS], DEAD)
            outs[first_pick // per][at + k : at + k + 1, :] = jnp.max(some, axis=0, keepdims=True)


def score(where, cand, pair, emb, sib, docs):
    total = cand.size
    docs = [d.reshape(-1, 4, DOC_ROWS, P_SIZE) for d in docs]
    return pl.pallas_call(
        score_body,
        out_shape=(jax.ShapeDtypeStruct((total, SEQ), f32),) * 2,
        in_specs=[SMEM] * 3 + vmem(2) + any_spec(4),
        out_specs=tuple(vmem(2)),
        scratch_shapes=[
            pltpu.VMEM((4, 4, 4, DOC_ROWS, P_SIZE), bf16),
            pltpu.SemaphoreType.DMA((4,)),
        ],
        compiler_params=params(8),
        cost_estimate=LIGHT,
        name="score",
    )(where, cand.reshape(-1), pair.reshape(-1), emb, sib, *docs[:3], *pinned(docs[3]))


def on_device(
    tokens,
    attend_weight,
    output_weight,
    attend_gain,
    up_weight,
    down_weight,
    mlp_gain,
    embed_weight,
    query_length,
    documents,
    document_length,
    candidates,
):
    req, mlp = lax.axis_index("req"), lax.axis_index("mlp")
    z, x, y, c = req // 4, req % 4, mlp // 2, mlp % 2
    where = jnp.stack([z, x, y, c, jnp.where(c == 0, x, z)]).astype(jnp.int32)
    start, query = first(
        where, up_weight, down_weight, documents.reshape(-1, P_SIZE), document_length, attend_weight
    )
    near = [send(start, way) for way in ("y+", "y-", "y2")]
    normed, low, high = attend(
        tokens, attend_weight, query, output_weight, attend_gain, query_length, up_weight, down_weight
    )
    pair = send(after(candidates, start), "c")
    near, pair = after((tuple(near), pair), normed)

    whole = [(k, 0, BLOCK) for k in range(3)] + [(3, PART, DOC_ROWS)]
    go = join([*near, start], whole, "join1")
    came = [send(go, way) for way in ("f+", "f-", "f2")]
    pair_normed = send(after(normed, go), "c")
    low_go = after(low, pair_normed)
    low_near = [send(low_go, "y+"), send(low_go, "y-")]
    sets = (normed, pair_normed)
    total = ffn(sets, (), [low, high], [(0, 0, 256), (1, 0, 256)], "ffn1")
    parts = [(i * BLOCK, SLICE) for i in range(3)]
    pieces = [(k, 0, SLICE) for k in range(3)] + [(3,) + p for p in parts]
    total = ffn(sets, total, [*near, came[0]], pieces, "ffn2")
    came, total = after((came, total), *total)
    takes = [(k, at, DOC_ROWS) for k in range(4) for at in [i * BLOCK + PART for i in range(3)] + [3 * BLOCK]]
    docs = join([go, *came], takes, "join2")
    last = [send(docs, way) for way in ("g+", "g-")]
    mid = 128
    low_near = after(tuple(low_near), docs)
    ahead = join([low_near[0]], [(0, k * 256, mid) for k in range(SLABS)], "join5")
    behind = join([low_near[1]], [(0, k * 256 + mid, mid) for k in range(SLABS)], "join6")
    low_far = [send(ahead, "y+"), send(behind, "y-")]
    pieces = [(k,) + p for k in range(2) for p in parts] + [(2, 0, 256), (3, 0, 256)]
    total = ffn(sets, total, [*came[1:], *low_near], pieces, "ffn3")
    far_docs = send(docs, "g2")
    low_far = after(tuple(low_far), *last)
    rest = [(0, 0, mid), (1, 0, mid)]
    away = ffn(sets[1:], total[1:], low_far, rest, "ffn4", split=2)
    other = [send(a, "c") for a in away]
    mine, = ffn(sets[:1], total[:1], low_far, rest, "ffn5")
    embedded, kept = embed(query_length, normed, mine, *other, mlp_gain, embed_weight)
    sib = send(after(kept, far_docs), "c")
    best, best_pair = score(where, candidates, pair, kept, sib, [docs, *last, far_docs])
    scores = final(best, send(best_pair, "c"), candidates.shape[0])
    return (embedded, scores)


def solution(mesh):
    return jax.shard_map(
        on_device,
        mesh=mesh,
        in_specs=(
            P(("req", "mlp"), None),
            P(),
            P(),
            P(),
            P(None, "mlp"),
            P(None, "mlp"),
            P(),
            P(),
            P(("req", "mlp")),
            P("req", "mlp", None),
            P("req"),
            P(("req", "mlp"), None),
        ),
        out_specs=(P(("req", "mlp"), None), P(("req", "mlp"), None)),
        check_vma=False,
    )
```

```python
import functools

import jax
import jax.numpy as jnp
from jax import lax
from jax.experimental import pallas as pl
from jax.experimental.pallas import tpu as pltpu
from jax.sharding import PartitionSpec as P

D = 1024
HEADS = 16
HD = 64
P_SIZE = 128
SEQ = 128
LANES = 128
SLABS = 2 * D // LANES
HALF = SLABS // 2
TOKS = 32
DOC_ROWS = 272
SLICE = 64
PART = SLABS * SLICE
BLOCK = PART + DOC_ROWS
AROUND = (0, 3, 1, 2)
AROUND_Y = (2, 3, 1, 0)
DEAD = -1e30
f32 = jnp.float32
bf16 = jnp.bfloat16


def dot(a, b):
    return jnp.dot(a, b, preferred_element_type=f32)


def dot_t(a, b):
    return lax.dot_general(a, b, (((1,), (1,)), ((), ())), preferred_element_type=f32)


def norm_rows(values, scaling):
    average = jnp.mean(values, axis=-1, keepdims=True)
    centred = values - average
    variance = jnp.mean(centred * centred, axis=-1, keepdims=True)
    return centred * lax.rsqrt(variance + 1e-05) * scaling


def gelu(x):
    return 0.5 * x * (1.0 + lax.erf(x * (0.5 ** 0.5)))


LIGHT = pl.CostEstimate(flops=1, transcendentals=0, bytes_accessed=1)


def params(mib):
    return pltpu.CompilerParams(vmem_limit_bytes=mib * 1024 * 1024)


def vmem(n=1):
    return [pl.BlockSpec(memory_space=pltpu.VMEM)] * n


def place(z, x, y, c):
    return ((z % 4) * 4 + x % 4) * 8 + (y % 4) * 2 + c % 2


def shift(move):
    return [
        (place(z, x, y, c), place(*move(z, x, y, c)))
        for z in range(4)
        for x in range(4)
        for y in range(4)
        for c in range(2)
    ]


def along_y(d):
    return shift(lambda z, x, y, c: (z, x, y + d, c))


def crossed(d, first):
    return shift(lambda z, x, y, c: (z, x + d, y, c) if c == first else (z + d, x, y, c))


STEPS = {"y+": along_y(1), "y-": along_y(-1), "y2": along_y(2)}
for name, d in (("+", 1), ("-", -1), ("2", 2)):
    STEPS["f" + name] = crossed(d, 0)
    STEPS["g" + name] = crossed(d, 1)
STEPS["c"] = shift(lambda z, x, y, c: (z, x, y, c + 1))


def send(value, way):
    return lax.ppermute(value, ("req", "mlp"), STEPS[way])


def after(value, *first):
    return lax.optimization_barrier((value, first))[0]


def any_spec(n=1):
    return [pl.BlockSpec(memory_space=pl.ANY)] * n


def pinned(*arrays):
    return [pltpu.with_memory_space_constraint(a, pltpu.HBM) for a in arrays]


def hbm(n=1):
    return [pl.BlockSpec(memory_space=pltpu.HBM)] * n


SMEM = pl.BlockSpec(memory_space=pltpu.SMEM)


def first_body(where, up, down, docs, lengths, qkv, out, query, held, turned, limits, sems):
    index = where[4]
    lanes = pl.ds(pl.multiple_of(256 + (index >> 1) * LANES, LANES), LANES)
    copies = [pltpu.make_async_copy(w.at[:, lanes], held.at[k], sems.at[k]) for k, w in enumerate((up, down))]
    tokens = DOC_ROWS - 16
    copies.append(pltpu.make_async_copy(docs, out.at[PART : PART + tokens], sems.at[2]))
    copies.append(pltpu.make_async_copy(lengths, limits, sems.at[3]))
    copies.append(pltpu.make_async_copy(qkv.at[:, :D], query, sems.at[4]))
    for copy in copies:
        copy.start()
    start = pl.multiple_of((index & 1) * SLICE, SLICE)
    for k in range(2):
        copies[k].wait()
        for j in range(HALF):
            slab = k * HALF + j
            turned[slab] = held[k, j * LANES : (j + 1) * LANES, :].T
            out[slab * SLICE : (slab + 1) * SLICE, :] = turned[slab, pl.ds(start, SLICE), :]
    copies[3].wait()
    row = lax.broadcasted_iota(jnp.int32, (16, LANES), 0)
    limit = jnp.zeros((16, LANES), f32)
    for j in range(8):
        limit = jnp.where(row == j, limits[j].astype(f32), limit)
    out[PART + tokens : BLOCK, :] = limit.astype(bf16)
    copies[2].wait()
    copies[4].wait()


def first(where, up, down, docs, lengths, qkv):
    return pl.pallas_call(
        first_body,
        out_shape=(jax.ShapeDtypeStruct((BLOCK, LANES), bf16), jax.ShapeDtypeStruct((D, D), bf16)),
        in_specs=[SMEM] + hbm(5),
        out_specs=tuple(vmem(2)),
        scratch_shapes=[
            pltpu.VMEM((2, D, LANES), bf16),
            pltpu.VMEM((SLABS, LANES, LANES), bf16),
            pltpu.SMEM((8,), jnp.int32),
            pltpu.SemaphoreType.DMA((5,)),
        ],
        compiler_params=params(8),
        cost_estimate=LIGHT,
        name="first",
    )(where, *pinned(up, down, docs, lengths, qkv))


def join_body(takes, *refs):
    out, at = refs[-1], 0
    for k, start, size in takes:
        out[at : at + size, :] = refs[k][start : start + size, :]
        at += size


def join(arrays, takes, name):
    return pl.pallas_call(
        functools.partial(join_body, takes),
        out_shape=jax.ShapeDtypeStruct((sum(t[2] for t in takes), LANES), bf16),
        in_specs=vmem(len(arrays)),
        out_specs=vmem()[0],
        compiler_params=params(16),
        cost_estimate=LIGHT,
        name=name,
    )(*arrays)


def norm_into(out, values, gain, block=32):
    for at in range(0, out.shape[0], block):
        rows = slice(at, at + block)
        out[rows, :] = norm_rows(values(rows), gain).astype(bf16)


def attend_body(
    length, qkv, wo_hbm, up, down, tok, query, gain, out, low_out, high_out, packed, context, held, wo, wide, added, sems
):
    rows_all = tok.shape[0]
    step = 512
    sources = [(qkv.at[:, D + c : D + c + step], held.at[:, c : c + step]) for c in range(0, 2 * D, step)]
    sources += [(up, wide.at[0]), (down, wide.at[1]), (wo_hbm, wo)]
    copies = [pltpu.make_async_copy(source, target, sems.at[i]) for i, (source, target) in enumerate(sources)]
    for copy in copies[:4]:
        copy.start()
    packed[:, :D] = dot(tok[...], query[...]).astype(bf16)
    for copy in copies[4:]:
        copy.start()
    for i in range(4):
        copies[i].wait()
        columns = slice(i * step, (i + 1) * step)
        packed[:, D + i * step : D + (i + 1) * step] = dot(tok[...], held[:, columns]).astype(bf16)
    for k in range(2):
        copies[4 + k].wait()
        for j in range(HALF):
            rows = slice(j * LANES, (j + 1) * LANES)
            low_out[k * HALF + j] = wide[k, rows, :256].T
            high_out[k * HALF + j] = wide[k, rows, 256:].T
    lane = lax.broadcasted_iota(jnp.int32, (2 * SEQ, LANES), 1)
    low = lax.broadcasted_iota(jnp.int32, (SEQ, LANES), 1) < HD

    def request(r, carry):
        rows = pl.ds(pl.multiple_of(r * SEQ, SEQ), SEQ)
        live = lane < length[r]
        for p in range(HEADS // 2):
            at = p * LANES
            q = packed[rows, at : at + LANES]
            k = packed[rows, D + at : D + at + LANES]
            v = packed[rows, 2 * D + at : 2 * D + at + LANES]
            zero = jnp.zeros_like(q)
            both = jnp.concatenate([jnp.where(low, q, zero), jnp.where(low, zero, q)], axis=0)
            logits = jnp.where(live, dot_t(both, k) * HD ** (-0.5), DEAD)
            weights = jnp.exp(logits - jnp.max(logits, axis=-1, keepdims=True))
            probs = (weights * (1.0 / jnp.sum(weights, axis=-1, keepdims=True))).astype(bf16)
            ctx = dot(probs, v)
            context[rows, at : at + LANES] = jnp.where(low, ctx[:SEQ], ctx[SEQ:]).astype(bf16)
        return carry

    lax.fori_loop(0, rows_all // SEQ, request, 0)
    copies[6].wait()
    added[...] = dot(context[...], wo[...])
    norm_into(out, lambda rows: tok[rows, :].astype(f32) + added[rows, :], gain[...])


def attend(tokens, qkv, query, wo, gain, length, up, down):
    rows = tokens.shape[0]
    piece = jax.ShapeDtypeStruct((SLABS, 256, LANES), bf16)
    normed, low, high = pl.pallas_call(
        attend_body,
        out_shape=(jax.ShapeDtypeStruct((rows, D), bf16), piece, piece),
        in_specs=[SMEM] + hbm(4) + vmem(3),
        out_specs=tuple(vmem(3)),
        scratch_shapes=[
            pltpu.VMEM((rows, 3 * D), bf16),
            pltpu.VMEM((rows, D), bf16),
            pltpu.VMEM((D, 2 * D), bf16),
            pltpu.VMEM((D, D), bf16),
            pltpu.VMEM((2, D, 512), bf16),
            pltpu.VMEM((rows, D), f32),
            pltpu.SemaphoreType.DMA((7,)),
        ],
        compiler_params=params(28),
        cost_estimate=LIGHT,
        name="attend",
    )(length, *pinned(qkv, wo, up, down), tokens, query, gain.reshape(1, D))
    return normed, low.reshape(-1, LANES), high.reshape(-1, LANES)


def halves_body(plus, minus, low, high, sems):
    rows = low.shape[0]
    copies = [
        pltpu.make_async_copy(plus.at[:rows], low, sems.at[0]),
        pltpu.make_async_copy(minus.at[rows:], high, sems.at[1]),
    ]
    for copy in copies:
        copy.start()
    for copy in copies:
        copy.wait()


def halves(plus, minus):
    half = jax.ShapeDtypeStruct((plus.shape[0] // 2, LANES), bf16)
    return pl.pallas_call(
        halves_body,
        out_shape=(half, half),
        in_specs=any_spec(2),
        out_specs=tuple(any_spec(2)),
        scratch_shapes=[pltpu.SemaphoreType.DMA((2,))],
        compiler_params=params(8),
        cost_estimate=LIGHT,
        name="halves",
    )(plus, minus)


def units(refs, half, start, size):
    slabs = []
    for j in range(HALF):
        parts, at = [], 0
        for ref, base, count in refs:
            low, high = max(start, at), min(start + size, at + count)
            if low < high:
                row = base + (half * HALF + j) * count
                parts.append(ref[row + low - at : row + high - at, :])
            at += count
        slabs.append(parts[0] if len(parts) == 1 else jnp.concatenate(parts, axis=0))
    return jnp.concatenate(slabs, axis=1)


def ffn_body(pieces, arrays, sets, fresh, *refs):
    inner, outs = refs[-1], refs[-1 - sets : -1]
    tokens, olds = refs[:sets], refs[sets : 2 * sets]
    held = refs[-1 - sets - arrays : -1 - sets]
    laid = [(held[k], base, count) for k, base, count in pieces]
    total = sum(count for _, _, count in pieces)
    for t in range(sets):
        x = tokens[t][...]
        for s in range(0, total, 256):
            n = min(256, total - s)
            inner[t, :, s : s + n] = gelu(dot_t(x, units(laid, 0, s, n))).astype(bf16)
    down = units(laid, 1, 0, total)
    for t in range(sets):
        for c in range(0, D, 256):
            more = dot(inner[t], down[:, c : c + 256])
            outs[t][:, c : c + 256] = more if fresh else olds[t][:, c : c + 256] + more


def ffn(tokens, olds, arrays, pieces, name):
    sets, rows = len(tokens), tokens[0].shape[0]
    total = sum(count for _, _, count in pieces)
    tail = tuple(tokens) + tuple(olds) + tuple(arrays)
    return pl.pallas_call(
        functools.partial(ffn_body, tuple(pieces), len(arrays), sets, not olds),
        out_shape=(jax.ShapeDtypeStruct((rows, D), f32),) * sets,
        in_specs=vmem(len(tail)),
        out_specs=tuple(vmem(sets)),
        input_output_aliases={sets + t: t for t in range(len(olds))},
        scratch_shapes=[pltpu.VMEM((sets, rows, total), bf16)],
        compiler_params=params(16),
        cost_estimate=LIGHT,
        name=name,
    )(*tail)


def embed_body(length, normed, mine, other, gain, we, out, kept, layer):
    norm_into(
        layer, lambda rows: normed[rows, :].astype(f32) + (mine[rows, :] + other[rows, :]), gain[...]
    )
    projected = dot(layer[...], we[...])
    unit = projected * lax.rsqrt(jnp.sum(projected * projected, axis=-1, keepdims=True) + 1e-06)
    slot = lax.broadcasted_iota(jnp.int32, (SEQ, P_SIZE), 0)
    for r in range(normed.shape[0] // SEQ):
        rows = slice(r * SEQ, (r + 1) * SEQ)
        live = jnp.where(slot < length[r], unit[rows], 0.0).astype(bf16)
        out[rows, :] = live
        kept[rows, :] = live


def embed(length, normed, mine, other, gain, we):
    shape = jax.ShapeDtypeStruct((normed.shape[0], P_SIZE), bf16)
    return pl.pallas_call(
        embed_body,
        out_shape=(shape, shape),
        in_specs=[SMEM] + vmem(5),
        out_specs=tuple(vmem(2)),
        scratch_shapes=[pltpu.VMEM(normed.shape, bf16)],
        compiler_params=params(12),
        cost_estimate=LIGHT,
        name="embed",
    )(length, normed, mine, other, gain.reshape(1, D), we)


def final_body(mine, other, out):
    out[...] = jnp.sum(jnp.maximum(mine[...], other[...]), axis=-1)


def final(mine, other, requests):
    picks = mine.shape[0] // requests
    shape = (requests, picks, mine.shape[1])
    return pl.pallas_call(
        final_body,
        out_shape=jax.ShapeDtypeStruct((requests, picks), f32),
        in_specs=vmem(2),
        out_specs=vmem()[0],
        compiler_params=params(8),
        cost_estimate=LIGHT,
        name="final",
    )(mine.reshape(shape), other.reshape(shape))


def score_body(where, cand, pair, emb, sib, *refs):
    docs, outs, held, sem = refs[:5], refs[5:7], refs[7], refs[8]
    copies = [
        pltpu.make_async_copy(docs[3 + i], held.at[3, 2 * i : 2 * i + 2], sem.at[i]) for i in range(2)
    ]
    for copy in copies:
        copy.start()
    for i in range(3):
        held[i] = docs[i][...]
    z, x, y, c = where[0], where[1], where[2], where[3]
    local = lax.broadcasted_iota(jnp.int32, (TOKS, LANES), 0)
    pos = jnp.concatenate(
        [local + TOKS * (2 * ((y + d) & 3) + c) for d in AROUND_Y], axis=0
    ).astype(f32)
    row = lax.broadcasted_iota(jnp.int32, (16, LANES), 0)

    def slot(d):
        return jnp.where(d == 0, 0, jnp.where(d == 3, 1, d + 1))

    for copy in copies:
        copy.wait()
    per = cand.shape[0]
    picks = 8
    for first_pick in range(0, 2 * per, picks):
        blocks, limits = [], []
        for i in range(first_pick, first_pick + picks):
            e = cand[i] if i < per else pair[i - per]
            j, req = e & 7, e >> 3
            sz, sx = slot(((req >> 2) - z) & 3), slot(((req & 3) - x) & 3)
            outer = jnp.where(c == 0, sz, sx)
            within = jnp.where(c == 0, sx, sz)
            block = held[outer, within, :, pl.ds(pl.multiple_of(j * TOKS, TOKS), TOKS), :]
            blocks.append(block.reshape(4 * TOKS, P_SIZE))
            lens = held[outer, within, 0, 8 * TOKS : DOC_ROWS, :].astype(f32)
            limits.append(jnp.sum(jnp.where(row == j, lens, 0.0), axis=0, keepdims=True))
        at = first_pick % per
        tokens = emb if first_pick < per else sib
        r = at // picks
        sims = dot_t(jnp.concatenate(blocks, axis=0), tokens[r * SEQ : (r + 1) * SEQ, :])
        for k in range(picks):
            some = jnp.where(pos < limits[k], sims[k * 4 * TOKS : (k + 1) * 4 * TOKS], DEAD)
            outs[first_pick // per][at + k : at + k + 1, :] = jnp.max(some, axis=0, keepdims=True)


def score(where, cand, pair, emb, sib, docs):
    total = cand.size
    docs = [d.reshape(-1, 4, DOC_ROWS, P_SIZE) for d in docs]
    return pl.pallas_call(
        score_body,
        out_shape=(jax.ShapeDtypeStruct((total, SEQ), f32),) * 2,
        in_specs=[SMEM] * 3 + vmem(5) + any_spec(2),
        out_specs=tuple(vmem(2)),
        scratch_shapes=[
            pltpu.VMEM((4, 4, 4, DOC_ROWS, P_SIZE), bf16),
            pltpu.SemaphoreType.DMA((2,)),
        ],
        compiler_params=params(8),
        cost_estimate=LIGHT,
        name="score",
    )(where, cand.reshape(-1), pair.reshape(-1), emb, sib, *docs)


def on_device(
    tokens,
    attend_weight,
    output_weight,
    attend_gain,
    up_weight,
    down_weight,
    mlp_gain,
    embed_weight,
    query_length,
    documents,
    document_length,
    candidates,
):
    req, mlp = lax.axis_index("req"), lax.axis_index("mlp")
    z, x, y, c = req // 4, req % 4, mlp // 2, mlp % 2
    where = jnp.stack([z, x, y, c, jnp.where(c == 0, x, z)]).astype(jnp.int32)
    start, query = first(
        where, up_weight, down_weight, documents.reshape(-1, P_SIZE), document_length, attend_weight
    )
    near = [send(start, way) for way in ("y2", "y+", "y-")]
    normed, low, high = attend(
        tokens, attend_weight, query, output_weight, attend_gain, query_length, up_weight, down_weight
    )
    pair = send(after(candidates, start), "c")
    near, pair = after((tuple(near), pair), normed)

    whole = [(k, 0, BLOCK) for k in range(3)] + [(3, PART, DOC_ROWS)]
    go = join([*near, start], whole, "join1")
    came = [send(go, way) for way in ("f+", "f-", "f2")]
    pair_normed = send(after(normed, go), "c")
    low_go = after(low, pair_normed)
    low_near = [send(low_go, "y+"), send(low_go, "y-")]
    sets = (normed, pair_normed)
    total = ffn(sets, (), [low, high], [(0, 0, 256), (1, 0, 256)], "ffn1")
    parts = [(i * BLOCK, SLICE) for i in range(3)]
    pieces = [(k, 0, SLICE) for k in range(3)] + [(3,) + p for p in parts]
    total = ffn(sets, total, [*near, came[0]], pieces, "ffn2")
    came, total = after((came, total), *total)
    takes = [(k, at, DOC_ROWS) for k in range(4) for at in [i * BLOCK + PART for i in range(3)] + [3 * BLOCK]]
    docs = join([go, *came], takes, "join2")
    last = [send(docs, way) for way in ("g+", "g-")]
    mid = 128
    low_near = after(tuple(low_near), docs)
    ahead = join([low_near[0]], [(0, k * 256, mid) for k in range(SLABS)], "join5")
    behind = join([low_near[1]], [(0, k * 256 + mid, mid) for k in range(SLABS)], "join6")
    low_far = [send(ahead, "y+"), send(behind, "y-")]
    pieces = [(k,) + p for k in range(2) for p in parts] + [(2, 0, 256), (3, 0, 256)]
    total = ffn(sets, total, [*came[1:], *low_near], pieces, "ffn3")
    parted = halves(*last)
    far_docs = [send(parted[0], "g+"), send(parted[1], "g-")]
    low_far = after(tuple(low_far), *parted)
    rest = [(0, 0, mid), (1, 0, mid)]
    away, = ffn(sets[1:], total[1:], low_far, rest, "ffn4")
    other = send(away, "c")
    mine, = ffn((normed,), total[:1], low_far, rest, "ffn5")
    embedded, kept = embed(query_length, normed, mine, other, mlp_gain, embed_weight)
    sib = send(kept, "c")
    best, best_pair = score(where, candidates, pair, kept, sib, [docs, *last, *far_docs])
    scores = final(best, send(best_pair, "c"), candidates.shape[0])
    return (embedded, scores)


def solution(mesh):
    return jax.shard_map(
        on_device,
        mesh=mesh,
        in_specs=(
            P(("req", "mlp"), None),
            P(),
            P(),
            P(),
            P(None, "mlp"),
            P(None, "mlp"),
            P(),
            P(),
            P(("req", "mlp")),
            P("req", "mlp", None),
            P("req"),
            P(("req", "mlp"), None),
        ),
        out_specs=(P(("req", "mlp"), None), P(("req", "mlp"), None)),
        check_vma=False,
    )
```

```python
import functools

import jax
import jax.numpy as jnp
from jax import lax
from jax.experimental import pallas as pl
from jax.experimental.pallas import tpu as pltpu
from jax.sharding import PartitionSpec as P

D = 1024
HEADS = 16
HD = 64
P_SIZE = 128
SEQ = 128
LANES = 128
SLABS = 2 * D // LANES
HALF = SLABS // 2
TOKS = 32
DOC_ROWS = 272
SLICE = 64
PART = SLABS * SLICE
BLOCK = PART + DOC_ROWS
AROUND = (0, 3, 1, 2)
AROUND_Y = (2, 3, 1, 0)
DEAD = -1e30
f32 = jnp.float32
bf16 = jnp.bfloat16


def dot(a, b):
    return jnp.dot(a, b, preferred_element_type=f32)


def dot_t(a, b):
    return lax.dot_general(a, b, (((1,), (1,)), ((), ())), preferred_element_type=f32)


def norm_rows(values, scaling):
    average = jnp.mean(values, axis=-1, keepdims=True)
    centred = values - average
    variance = jnp.mean(centred * centred, axis=-1, keepdims=True)
    return centred * lax.rsqrt(variance + 1e-05) * scaling


def gelu(x):
    return 0.5 * x * (1.0 + lax.erf(x * (0.5 ** 0.5)))


LIGHT = pl.CostEstimate(flops=1, transcendentals=0, bytes_accessed=1)


def params(mib):
    return pltpu.CompilerParams(vmem_limit_bytes=mib * 1024 * 1024)


def vmem(n=1):
    return [pl.BlockSpec(memory_space=pltpu.VMEM)] * n


def place(z, x, y, c):
    return ((z % 4) * 4 + x % 4) * 8 + (y % 4) * 2 + c % 2


def shift(move):
    return [
        (place(z, x, y, c), place(*move(z, x, y, c)))
        for z in range(4)
        for x in range(4)
        for y in range(4)
        for c in range(2)
    ]


def along_y(d):
    return shift(lambda z, x, y, c: (z, x, y + d, c))


def crossed(d, first):
    return shift(lambda z, x, y, c: (z, x + d, y, c) if c == first else (z + d, x, y, c))


STEPS = {"y+": along_y(1), "y-": along_y(-1), "y2": along_y(2)}
for name, d in (("+", 1), ("-", -1), ("2", 2)):
    STEPS["f" + name] = crossed(d, 0)
    STEPS["g" + name] = crossed(d, 1)
STEPS["c"] = shift(lambda z, x, y, c: (z, x, y, c + 1))


def send(value, way):
    return lax.ppermute(value, ("req", "mlp"), STEPS[way])


def after(value, *first):
    return lax.optimization_barrier((value, first))[0]


def any_spec(n=1):
    return [pl.BlockSpec(memory_space=pl.ANY)] * n


def pinned(*arrays):
    return [pltpu.with_memory_space_constraint(a, pltpu.HBM) for a in arrays]


def hbm(n=1):
    return [pl.BlockSpec(memory_space=pltpu.HBM)] * n


SMEM = pl.BlockSpec(memory_space=pltpu.SMEM)


def first_body(where, up, down, docs, lengths, out, held, turned, limits, sems):
    index = where[4]
    lanes = pl.ds(pl.multiple_of(256 + (index >> 1) * LANES, LANES), LANES)
    copies = [pltpu.make_async_copy(w.at[:, lanes], held.at[k], sems.at[k]) for k, w in enumerate((up, down))]
    tokens = DOC_ROWS - 16
    copies.append(pltpu.make_async_copy(docs, out.at[PART : PART + tokens], sems.at[2]))
    copies.append(pltpu.make_async_copy(lengths, limits, sems.at[3]))
    for copy in copies:
        copy.start()
    start = pl.multiple_of((index & 1) * SLICE, SLICE)
    for k in range(2):
        copies[k].wait()
        for j in range(HALF):
            slab = k * HALF + j
            turned[slab] = held[k, j * LANES : (j + 1) * LANES, :].T
            out[slab * SLICE : (slab + 1) * SLICE, :] = turned[slab, pl.ds(start, SLICE), :]
    copies[3].wait()
    row = lax.broadcasted_iota(jnp.int32, (16, LANES), 0)
    limit = jnp.zeros((16, LANES), f32)
    for j in range(8):
        limit = jnp.where(row == j, limits[j].astype(f32), limit)
    out[PART + tokens : BLOCK, :] = limit.astype(bf16)
    copies[2].wait()


def first(where, up, down, docs, lengths):
    return pl.pallas_call(
        first_body,
        out_shape=jax.ShapeDtypeStruct((BLOCK, LANES), bf16),
        in_specs=[SMEM] + hbm(4),
        out_specs=vmem()[0],
        scratch_shapes=[
            pltpu.VMEM((2, D, LANES), bf16),
            pltpu.VMEM((SLABS, LANES, LANES), bf16),
            pltpu.SMEM((8,), jnp.int32),
            pltpu.SemaphoreType.DMA((4,)),
        ],
        compiler_params=params(8),
        cost_estimate=LIGHT,
        name="first",
    )(where, *pinned(up, down, docs, lengths))


def join_body(takes, *refs):
    out, at = refs[-1], 0
    for k, start, size in takes:
        out[at : at + size, :] = refs[k][start : start + size, :]
        at += size


def join(arrays, takes, name):
    return pl.pallas_call(
        functools.partial(join_body, takes),
        out_shape=jax.ShapeDtypeStruct((sum(t[2] for t in takes), LANES), bf16),
        in_specs=vmem(len(arrays)),
        out_specs=vmem()[0],
        compiler_params=params(16),
        cost_estimate=LIGHT,
        name=name,
    )(*arrays)


def norm_into(out, values, gain, block=32):
    for at in range(0, out.shape[0], block):
        rows = slice(at, at + block)
        out[rows, :] = norm_rows(values(rows), gain).astype(bf16)


def attend_body(
    length, qkv, wo_hbm, up, down, tok, gain, out, low_out, high_out, packed, context, held, wo, wide, added, sems
):
    rows_all = tok.shape[0]
    step = 512
    sources = [(qkv.at[:, c : c + step], held.at[:, c : c + step]) for c in range(0, 3 * D, step)]
    sources += [(up, wide.at[0]), (down, wide.at[1]), (wo_hbm, wo)]
    copies = [pltpu.make_async_copy(source, target, sems.at[i]) for i, (source, target) in enumerate(sources)]
    for copy in copies[:3]:
        copy.start()
    for i in range(6):
        copies[i].wait()
        copies[3 + i].start()
        columns = slice(i * step, (i + 1) * step)
        packed[:, columns] = dot(tok[...], held[:, columns]).astype(bf16)
    for k in range(2):
        copies[6 + k].wait()
        for j in range(HALF):
            rows = slice(j * LANES, (j + 1) * LANES)
            low_out[k * HALF + j] = wide[k, rows, :256].T
            high_out[k * HALF + j] = wide[k, rows, 256:].T
    key = lax.broadcasted_iota(jnp.int32, (SEQ, 2 * LANES), 0)
    low = lax.broadcasted_iota(jnp.int32, (SEQ, LANES), 1) < HD

    def request(r, carry):
        rows = pl.ds(pl.multiple_of(r * SEQ, SEQ), SEQ)
        live = key < length[r]
        for p in range(HEADS // 2):
            at = p * LANES
            q = packed[rows, at : at + LANES]
            k = packed[rows, D + at : D + at + LANES]
            v = packed[rows, 2 * D + at : 2 * D + at + LANES]
            zero = jnp.zeros_like(q)
            both = jnp.concatenate([jnp.where(low, q, zero), jnp.where(low, zero, q)], axis=0)
            logits = jnp.where(live, dot_t(k, both) * HD ** (-0.5), DEAD)
            weights = jnp.exp(logits - jnp.max(logits, axis=0, keepdims=True))
            probs = (weights * (1.0 / jnp.sum(weights, axis=0, keepdims=True))).astype(bf16)
            ctx = lax.dot_general(probs, v, (((0,), (0,)), ((), ())), preferred_element_type=f32)
            context[rows, at : at + LANES] = jnp.where(low, ctx[:SEQ], ctx[SEQ:]).astype(bf16)
        return carry

    lax.fori_loop(0, rows_all // SEQ, request, 0, unroll=True)
    copies[8].wait()
    added[...] = dot(context[...], wo[...])
    norm_into(out, lambda rows: tok[rows, :].astype(f32) + added[rows, :], gain[...])


def attend(tokens, qkv, wo, gain, length, up, down):
    rows = tokens.shape[0]
    piece = jax.ShapeDtypeStruct((SLABS, 256, LANES), bf16)
    normed, low, high = pl.pallas_call(
        attend_body,
        out_shape=(jax.ShapeDtypeStruct((rows, D), bf16), piece, piece),
        in_specs=[SMEM] + hbm(4) + vmem(2),
        out_specs=tuple(vmem(3)),
        scratch_shapes=[
            pltpu.VMEM((rows, 3 * D), bf16),
            pltpu.VMEM((rows, D), bf16),
            pltpu.VMEM((D, 3 * D), bf16),
            pltpu.VMEM((D, D), bf16),
            pltpu.VMEM((2, D, 512), bf16),
            pltpu.VMEM((rows, D), f32),
            pltpu.SemaphoreType.DMA((9,)),
        ],
        compiler_params=params(28),
        cost_estimate=LIGHT,
        name="attend",
    )(length, *pinned(qkv, wo, up, down), tokens, gain.reshape(1, D))
    return normed, low.reshape(-1, LANES), high.reshape(-1, LANES)


def halves_body(plus, minus, low, high, sems):
    rows = low.shape[0]
    copies = [
        pltpu.make_async_copy(plus.at[:rows], low, sems.at[0]),
        pltpu.make_async_copy(minus.at[rows:], high, sems.at[1]),
    ]
    for copy in copies:
        copy.start()
    for copy in copies:
        copy.wait()


def halves(plus, minus):
    half = jax.ShapeDtypeStruct((plus.shape[0] // 2, LANES), bf16)
    return pl.pallas_call(
        halves_body,
        out_shape=(half, half),
        in_specs=any_spec(2),
        out_specs=tuple(any_spec(2)),
        scratch_shapes=[pltpu.SemaphoreType.DMA((2,))],
        compiler_params=params(8),
        cost_estimate=LIGHT,
        name="halves",
    )(plus, minus)


def units(refs, half, start, size):
    slabs = []
    for j in range(HALF):
        parts, at = [], 0
        for ref, base, count in refs:
            low, high = max(start, at), min(start + size, at + count)
            if low < high:
                row = base + (half * HALF + j) * count
                parts.append(ref[row + low - at : row + high - at, :])
            at += count
        slabs.append(parts[0] if len(parts) == 1 else jnp.concatenate(parts, axis=0))
    return jnp.concatenate(slabs, axis=1)


def ffn_body(pieces, arrays, sets, fresh, *refs):
    inner, outs = refs[-1], refs[-1 - sets : -1]
    tokens, olds = refs[:sets], refs[sets : 2 * sets]
    held = refs[-1 - sets - arrays : -1 - sets]
    laid = [(held[k], base, count) for k, base, count in pieces]
    total = sum(count for _, _, count in pieces)
    for t in range(sets):
        x = tokens[t][...]
        for s in range(0, total, 256):
            n = min(256, total - s)
            inner[t, :, s : s + n] = gelu(dot_t(x, units(laid, 0, s, n))).astype(bf16)
    down = units(laid, 1, 0, total)
    for t in range(sets):
        for c in range(0, D, 256):
            more = dot(inner[t], down[:, c : c + 256])
            outs[t][:, c : c + 256] = more if fresh else olds[t][:, c : c + 256] + more


def ffn(tokens, olds, arrays, pieces, name):
    sets, rows = len(tokens), tokens[0].shape[0]
    total = sum(count for _, _, count in pieces)
    tail = tuple(tokens) + tuple(olds) + tuple(arrays)
    return pl.pallas_call(
        functools.partial(ffn_body, tuple(pieces), len(arrays), sets, not olds),
        out_shape=(jax.ShapeDtypeStruct((rows, D), f32),) * sets,
        in_specs=vmem(len(tail)),
        out_specs=tuple(vmem(sets)),
        input_output_aliases={sets + t: t for t in range(len(olds))},
        scratch_shapes=[pltpu.VMEM((sets, rows, total), bf16)],
        compiler_params=params(16),
        cost_estimate=LIGHT,
        name=name,
    )(*tail)


def embed_body(length, normed, mine, other, gain, we, out, kept, layer):
    norm_into(
        layer, lambda rows: normed[rows, :].astype(f32) + (mine[rows, :] + other[rows, :]), gain[...]
    )
    projected = dot(layer[...], we[...])
    unit = projected * lax.rsqrt(jnp.sum(projected * projected, axis=-1, keepdims=True) + 1e-06)
    slot = lax.broadcasted_iota(jnp.int32, (SEQ, P_SIZE), 0)
    for r in range(normed.shape[0] // SEQ):
        rows = slice(r * SEQ, (r + 1) * SEQ)
        live = jnp.where(slot < length[r], unit[rows], 0.0).astype(bf16)
        out[rows, :] = live
        kept[rows, :] = live


def embed(length, normed, mine, other, gain, we):
    shape = jax.ShapeDtypeStruct((normed.shape[0], P_SIZE), bf16)
    return pl.pallas_call(
        embed_body,
        out_shape=(shape, shape),
        in_specs=[SMEM] + vmem(5),
        out_specs=tuple(vmem(2)),
        scratch_shapes=[pltpu.VMEM(normed.shape, bf16)],
        compiler_params=params(12),
        cost_estimate=LIGHT,
        name="embed",
    )(length, normed, mine, other, gain.reshape(1, D), we)


def final_body(mine, other, out):
    out[...] = jnp.sum(jnp.maximum(mine[...], other[...]), axis=-1)


def final(mine, other, requests):
    picks = mine.shape[0] // requests
    shape = (requests, picks, mine.shape[1])
    return pl.pallas_call(
        final_body,
        out_shape=jax.ShapeDtypeStruct((requests, picks), f32),
        in_specs=vmem(2),
        out_specs=vmem()[0],
        compiler_params=params(8),
        cost_estimate=LIGHT,
        name="final",
    )(mine.reshape(shape), other.reshape(shape))


def score_body(where, cand, pair, emb, sib, *refs):
    docs, outs, held, sem = refs[:5], refs[5:7], refs[7], refs[8]
    copies = [
        pltpu.make_async_copy(docs[3 + i], held.at[3, 2 * i : 2 * i + 2], sem.at[i]) for i in range(2)
    ]
    for copy in copies:
        copy.start()
    for i in range(3):
        held[i] = docs[i][...]
    z, x, y, c = where[0], where[1], where[2], where[3]
    local = lax.broadcasted_iota(jnp.int32, (TOKS, LANES), 0)
    pos = jnp.concatenate(
        [local + TOKS * (2 * ((y + d) & 3) + c) for d in AROUND_Y], axis=0
    ).astype(f32)
    row = lax.broadcasted_iota(jnp.int32, (16, LANES), 0)

    def slot(d):
        return jnp.where(d == 0, 0, jnp.where(d == 3, 1, d + 1))

    for copy in copies:
        copy.wait()
    per = cand.shape[0]
    picks = 8
    for first_pick in range(0, 2 * per, picks):
        blocks, limits = [], []
        for i in range(first_pick, first_pick + picks):
            e = cand[i] if i < per else pair[i - per]
            j, req = e & 7, e >> 3
            sz, sx = slot(((req >> 2) - z) & 3), slot(((req & 3) - x) & 3)
            outer = jnp.where(c == 0, sz, sx)
            within = jnp.where(c == 0, sx, sz)
            block = held[outer, within, :, pl.ds(pl.multiple_of(j * TOKS, TOKS), TOKS), :]
            blocks.append(block.reshape(4 * TOKS, P_SIZE))
            lens = held[outer, within, 0, 8 * TOKS : DOC_ROWS, :].astype(f32)
            limits.append(jnp.sum(jnp.where(row == j, lens, 0.0), axis=0, keepdims=True))
        at = first_pick % per
        tokens = emb if first_pick < per else sib
        r = at // picks
        sims = dot_t(jnp.concatenate(blocks, axis=0), tokens[r * SEQ : (r + 1) * SEQ, :])
        for k in range(picks):
            some = jnp.where(pos < limits[k], sims[k * 4 * TOKS : (k + 1) * 4 * TOKS], DEAD)
            outs[first_pick // per][at + k : at + k + 1, :] = jnp.max(some, axis=0, keepdims=True)


def score(where, cand, pair, emb, sib, docs):
    total = cand.size
    docs = [d.reshape(-1, 4, DOC_ROWS, P_SIZE) for d in docs]
    return pl.pallas_call(
        score_body,
        out_shape=(jax.ShapeDtypeStruct((total, SEQ), f32),) * 2,
        in_specs=[SMEM] * 3 + vmem(5) + any_spec(2),
        out_specs=tuple(vmem(2)),
        scratch_shapes=[
            pltpu.VMEM((4, 4, 4, DOC_ROWS, P_SIZE), bf16),
            pltpu.SemaphoreType.DMA((2,)),
        ],
        compiler_params=params(8),
        cost_estimate=LIGHT,
        name="score",
    )(where, cand.reshape(-1), pair.reshape(-1), emb, sib, *docs)


def on_device(
    tokens,
    attend_weight,
    output_weight,
    attend_gain,
    up_weight,
    down_weight,
    mlp_gain,
    embed_weight,
    query_length,
    documents,
    document_length,
    candidates,
):
    req, mlp = lax.axis_index("req"), lax.axis_index("mlp")
    z, x, y, c = req // 4, req % 4, mlp // 2, mlp % 2
    where = jnp.stack([z, x, y, c, jnp.where(c == 0, x, z)]).astype(jnp.int32)
    start = first(where, up_weight, down_weight, documents.reshape(-1, P_SIZE), document_length)
    near = [send(start, way) for way in ("y2", "y+", "y-")]
    normed, low, high = attend(
        tokens, attend_weight, output_weight, after(attend_gain, start), query_length, up_weight, down_weight
    )
    pair = send(after(candidates, start), "c")
    near, pair = after((tuple(near), pair), normed)

    whole = [(k, 0, BLOCK) for k in range(3)] + [(3, PART, DOC_ROWS)]
    go = join([*near, start], whole, "join1")
    came = [send(go, way) for way in ("f+", "f-", "f2")]
    pair_normed = send(after(normed, go), "c")
    low_go = after(low, pair_normed)
    low_near = [send(low_go, "y+"), send(low_go, "y-")]
    sets = (normed, pair_normed)
    total = ffn(sets, (), [low, high], [(0, 0, 256), (1, 0, 256)], "ffn1")
    parts = [(i * BLOCK, SLICE) for i in range(3)]
    pieces = [(k, 0, SLICE) for k in range(3)] + [(3,) + p for p in parts]
    total = ffn(sets, total, [*near, came[0]], pieces, "ffn2")
    came, total = after((came, total), *total)
    takes = [(k, at, DOC_ROWS) for k in range(4) for at in [i * BLOCK + PART for i in range(3)] + [3 * BLOCK]]
    docs = join([go, *came], takes, "join2")
    last = [send(docs, way) for way in ("g+", "g-")]
    mid = 128
    low_near = after(tuple(low_near), docs)
    ahead = join([low_near[0]], [(0, k * 256, mid) for k in range(SLABS)], "join5")
    behind = join([low_near[1]], [(0, k * 256 + mid, mid) for k in range(SLABS)], "join6")
    low_far = [send(ahead, "y+"), send(behind, "y-")]
    pieces = [(k,) + p for k in range(2) for p in parts] + [(2, 0, 256), (3, 0, 256)]
    total = ffn(sets, total, [*came[1:], *low_near], pieces, "ffn3")
    parted = halves(*last)
    far_docs = [send(parted[0], "g+"), send(parted[1], "g-")]
    low_far = after(tuple(low_far), *parted)
    rest = [(0, 0, mid), (1, 0, mid)]
    away, = ffn(sets[1:], total[1:], low_far, rest, "ffn4")
    other = send(away, "c")
    mine, = ffn((normed,), total[:1], low_far, rest, "ffn5")
    embedded, kept = embed(query_length, normed, mine, other, mlp_gain, embed_weight)
    sib = send(kept, "c")
    best, best_pair = score(where, candidates, pair, kept, sib, [docs, *last, *far_docs])
    scores = final(best, send(best_pair, "c"), candidates.shape[0])
    return (embedded, scores)


def solution(mesh):
    return jax.shard_map(
        on_device,
        mesh=mesh,
        in_specs=(
            P(("req", "mlp"), None),
            P(),
            P(),
            P(),
            P(None, "mlp"),
            P(None, "mlp"),
            P(),
            P(),
            P(("req", "mlp")),
            P("req", "mlp", None),
            P("req"),
            P(("req", "mlp"), None),
        ),
        out_specs=(P(("req", "mlp"), None), P(("req", "mlp"), None)),
        check_vma=False,
    )
```
